512 devices in a mesh: facet: 32 (over z_lo, y, core), strip: 16 (over x, z_hi).
Axes of the slice: x: 4, y: 8, z: 8 (z_hi: 4, z_lo: 2; z = z_hi * 2 + z_lo), core: 2. Of those that a mesh axis runs over, the one named last changes fastest.
Arguments:
- facet_pixels: bfloat16 [2, 32, 2048, 4096], P(None, 'facet', 'strip'), may hold values from -6 to 6
- facet_offsets: int32 [32, 2], P('facet'), may hold values from 0 to 65535
- subgrid_offsets: int32 [2, 2], replicated, may hold values from 0 to 65023
Outputs:
- subgrid: float32 [512, 2, 2, 512], P('strip', None, None, 'facet')
The draws below stay inside these ranges and needn't reach their ends.
All inputs are finite; a program needn't handle non-finite values.
Results may differ from the reference program's by a relative error of at most 0.0074.
Values may be sent and summed in bfloat16 or wider, within the bound.
No kernel may reach another device: no remote copies, remote signals or barrier semaphores. Data moves between devices by JAX's collectives and lax.ppermute only.
A program may use at most 64 MiB of HBM per device.

```python
import math
import jax
import jax.numpy as jnp
from jax import lax

IMAGE_N = 65536
FACET_W = 4096
FREQ = 512
ROW_FREQ = 512
COLUMNS = 2
FACETS = 32
FACET_ROWS = 2048


def set_ends(entries, stream_key, low, top_value):
    longest = entries.shape.index(max(entries.shape))
    spots = []
    for shift in (0, 1):
        where = [jax.random.randint(jax.random.fold_in(stream_key, axis), (), 0, length) for axis, length in enumerate(entries.shape)]
        where[longest] = (where[longest] + shift) % entries.shape[longest]
        spots.append(tuple(where))
    return entries.at[spots[0]].set(low).at[spots[1]].set(top_value)


def levels(key, dims, pieces, low, largest):
    factor_of = 1.0
    for axis_at, parts in pieces:
        steps = jax.random.uniform(jax.random.fold_in(jax.random.fold_in(key, 6), axis_at), (parts,), jnp.float32, low / len(pieces), largest / len(pieces))
        factor_of = factor_of * jnp.repeat(jnp.exp(steps), dims[axis_at] // parts).reshape((-1,) + (1,) * (len(dims) - 1 - axis_at))
    return factor_of


def normal_values(key, shape, width, reach, split=(), kind=jnp.bfloat16):
    drawn = jax.random.normal(key, shape, jnp.float32) * width
    if len(split) > 0:
        drawn = levels(key, shape, split, -0.22, 0.18) * drawn
    return jnp.clip(drawn, min=-reach, max=reach).astype(kind)


def setup_inputs(seed: int = 0) -> dict:
    arg_keys = jax.random.split(jax.random.key(seed), 4)
    return {
        "facet_pixels": normal_values(arg_keys[0], (2, FACETS, FACET_ROWS, FACET_W), 1.0, 6.0, ((1, 32), (2, 16))),
        "facet_offsets": set_ends(jax.random.randint(arg_keys[1], (FACETS, 2), 0, IMAGE_N), jax.random.fold_in(arg_keys[1], 1), 0, IMAGE_N - 1).astype(jnp.int32),
        "subgrid_offsets": set_ends(jax.random.randint(arg_keys[2], (COLUMNS, 2), 0, IMAGE_N - max(FREQ, ROW_FREQ)), jax.random.fold_in(arg_keys[2], 1), 0, (IMAGE_N - max(FREQ, ROW_FREQ)) - 1).astype(jnp.int32),
    }


def phase_mod(offset, freq, modulus):
    high = offset // 256
    low = offset % 256
    return (high * (256 * freq % modulus) + low * freq) % modulus

def twiddle(product, modulus):
    angle = 2.0 * math.pi / modulus * product.astype(jnp.float32)
    return (jnp.cos(angle), -jnp.sin(angle))

def bf_tables(product, modulus):
    cosine, sine = twiddle(product, modulus)
    return (cosine.astype(jnp.bfloat16), sine.astype(jnp.bfloat16), (cosine + sine).astype(jnp.bfloat16))

def reference(facet_pixels, facet_offsets, subgrid_offsets):
    col_freq = subgrid_offsets[:, 0][:, None] + jnp.arange(FREQ, dtype=jnp.int32)[None, :]
    row_freq = subgrid_offsets[:, 1][:, None] + jnp.arange(ROW_FREQ, dtype=jnp.int32)[None, :]
    pixel_col = jnp.arange(FACET_W, dtype=jnp.int32)
    col_product = (pixel_col[:, None, None] * col_freq[None, :, :] % IMAGE_N).reshape(FACET_W, COLUMNS * FREQ)
    col_tables = bf_tables(col_product, IMAGE_N)
    pixel_row = jnp.arange(FACET_ROWS, dtype=jnp.int32)
    row_product = row_freq[:, :, None] * pixel_row[None, None, :] % IMAGE_N
    row_tables = bf_tables(row_product, IMAGE_N)
    scale = 1.0 / math.sqrt(FACET_W * FACET_ROWS * FACETS)

    def one_facet(index, running):
        pixels = lax.dynamic_index_in_dim(facet_pixels, index, 1, keepdims=False)
        offsets = lax.dynamic_index_in_dim(facet_offsets, index, 0, keepdims=False)
        pixels_real = pixels[0]
        pixels_imag = pixels[1]
        pixel_sum = (pixels_real.astype(jnp.float32) + pixels_imag.astype(jnp.float32)).astype(jnp.bfloat16)
        term_one = jnp.dot(pixels_real, col_tables[0], preferred_element_type=jnp.float32)
        term_two = jnp.dot(pixels_imag, col_tables[1], preferred_element_type=jnp.float32)
        term_three = jnp.dot(pixel_sum, col_tables[2], preferred_element_type=jnp.float32)
        y_real = (term_one - term_two).astype(jnp.bfloat16)
        y_imag = (term_three - term_one - term_two).astype(jnp.bfloat16)
        y_real, y_imag = lax.optimization_barrier((y_real, y_imag))
        y_sum = (y_real.astype(jnp.float32) + y_imag.astype(jnp.float32)).astype(jnp.bfloat16)
        y_real = y_real.reshape(FACET_ROWS, COLUMNS, FREQ).astype(jnp.float32)
        y_imag = y_imag.reshape(FACET_ROWS, COLUMNS, FREQ).astype(jnp.float32)
        y_sum = y_sum.reshape(FACET_ROWS, COLUMNS, FREQ).astype(jnp.float32)
        part_one = jnp.einsum('cir,rcm->icm', row_tables[0].astype(jnp.float32), y_real)
        part_two = jnp.einsum('cir,rcm->icm', row_tables[1].astype(jnp.float32), y_imag)
        part_three = jnp.einsum('cir,rcm->icm', row_tables[2].astype(jnp.float32), y_sum)
        z_real = part_one - part_two
        z_imag = part_three - part_one - part_two
        col_part = phase_mod(offsets[0], col_freq, IMAGE_N)
        row_part = phase_mod(offsets[1], row_freq, IMAGE_N)
        total = jnp.transpose((row_part[:, :, None] + col_part[:, None, :]) % IMAGE_N, (1, 0, 2))
        cosine, sine = twiddle(total, IMAGE_N)
        out_real = scale * (z_real * cosine - z_imag * sine)
        out_imag = scale * (z_real * sine + z_imag * cosine)
        return running + jnp.stack([out_real, out_imag], axis=1)
    start_value = jnp.zeros((ROW_FREQ, 2, COLUMNS, FREQ), jnp.float32)
    return lax.fori_loop(0, FACETS, one_facet, start_value)
```

```python
import math

import jax
import jax.numpy as jnp
from jax import lax
from jax.experimental import pallas as pl
from jax.experimental.pallas import tpu as pltpu
from jax.sharding import PartitionSpec as P

TURN = 131072
HALF = 256
FREQ = 512
COLUMNS = 2
ROWS = 128
WIDTH = 4096
BLOCKS = 8
BLOCK = WIDTH // BLOCKS
CHUNK_ROWS = 72
F32 = jnp.float32
BF16 = jnp.bfloat16


def cos_turn(t):
    v = jnp.abs((t & (TURN - 1)) - TURN // 2) - TURN // 4
    z = v.astype(F32) * (2.0 * math.pi / TURN)
    q = z * z
    p = -1.0 / 39916800.0
    for term in (1.0 / 362880.0, -1.0 / 5040.0, 1.0 / 120.0, -1.0 / 6.0):
        p = p * q + term
    return z + z * (q * p)


def sin_turn(t):
    return cos_turn(t - TURN // 4)


def iota(shape, axis):
    return lax.broadcasted_iota(jnp.int32, shape, axis)


def column_kernel(x_hbm, facet_ref, sub_ref, out_ref, x_ref, xp_ref, tb_ref, acc_ref, e2_ref, e1_ref, tw_ref, sems):
    strip = lax.axis_index("strip")
    copies = [
        pltpu.make_async_copy(
            x_hbm.at[:, 0, :, pl.ds(b * BLOCK, BLOCK)],
            x_ref.at[:, :, pl.ds(b * BLOCK, BLOCK)],
            sems.at[b],
        )
        for b in range(BLOCKS)
    ]
    for copy in copies:
        copy.start()
    fx = facet_ref[0, 0]
    fy = facet_ref[0, 1]
    odd = 2 * iota((ROWS, HALF), 1) + 1
    e2_t = iota((ROWS, HALF), 0) * odd
    e2_ref[0] = cos_turn(e2_t)
    e2_ref[1] = sin_turn(e2_t)
    e1_t = iota((32, HALF), 0) * 128 * (2 * iota((32, HALF), 1) + 1)
    e1_ref[0] = cos_turn(e1_t)
    e1_ref[1] = sin_turn(e1_t)
    row = iota((8, WIDTH), 0)
    centre = jnp.where(row % 2 == 0, 2 * sub_ref[0, 0] + 511, 2 * sub_ref[1, 0] + 511)
    tw_ref[...] = cos_turn(iota((8, WIDTH), 1) * centre - jnp.where(row >= 2, TURN // 4, 0))

    def prepare(b):
        copies[b].wait()
        slot = b % 2
        for n in range(BLOCK // 128):
            lo = b * BLOCK + n * 128
            xr = x_ref[0, :, lo : lo + 128].astype(F32)
            xi = x_ref[1, :, lo : lo + 128].astype(F32)
            for c in range(COLUMNS):
                wc = tw_ref[c : c + 1, lo : lo + 128]
                ws = tw_ref[2 + c : 3 + c, lo : lo + 128]
                base = c * 2 * ROWS
                xp_ref[slot, base : base + ROWS, n * 128 : n * 128 + 128] = (xr * wc + xi * ws).astype(BF16)
                xp_ref[slot, base + ROWS : base + 2 * ROWS, n * 128 : n * 128 + 128] = (xi * wc - xr * ws).astype(BF16)
            a = lo // 128
            c1 = e1_ref[0, a : a + 1, :]
            s1 = e1_ref[1, a : a + 1, :]
            c2 = e2_ref[0]
            s2 = e2_ref[1]
            tb_ref[slot, n * 128 : n * 128 + 128, :HALF] = (c1 * c2 - s1 * s2).astype(BF16)
            tb_ref[slot, n * 128 : n * 128 + 128, HALF:] = (s1 * c2 + c1 * s2).astype(BF16)

    prepare(0)
    for b in range(BLOCKS):
        if b + 1 < BLOCKS:
            prepare(b + 1)
        part = jnp.dot(xp_ref[b % 2], tb_ref[b % 2], preferred_element_type=F32)
        if b == 0:
            acc_ref[...] = part
        else:
            acc_ref[...] += part

    psi_t = fx * (2 * iota((8, HALF), 1) + 1)
    cpsi = cos_turn(psi_t)[0:1]
    spsi = sin_turn(psi_t)[0:1]
    scale = 1.0 / 16384.0
    for c in range(COLUMNS):
        phi_t = (fy + strip * ROWS + iota((ROWS, HALF), 0)) * (2 * sub_ref[c, 1] + 511) + fx * (
            2 * sub_ref[c, 0] + 511
        )
        cphi = cos_turn(phi_t) * scale
        sphi = sin_turn(phi_t) * scale
        base = c * 2 * ROWS
        cr = acc_ref[base : base + ROWS, :HALF]
        sr = acc_ref[base : base + ROWS, HALF:]
        ci = acc_ref[base + ROWS : base + 2 * ROWS, :HALF]
        si = acc_ref[base + ROWS : base + 2 * ROWS, HALF:]
        for sign in (1, -1):
            if sign > 0:
                yr, yi = cr + si, ci - sr
                pc = cphi * cpsi - sphi * spsi
                ps = sphi * cpsi + cphi * spsi
            else:
                yr, yi = cr - si, ci + sr
                pc = cphi * cpsi + sphi * spsi
                ps = sphi * cpsi - cphi * spsi
            for part, value in enumerate((yr * pc + yi * ps, yi * pc - yr * ps)):
                turned = value.T.astype(BF16)
                at = (part * 2 + c) * 16
                for t in range(16):
                    to = 16 + t if sign > 0 else 15 - t
                    out_ref[to, at : at + 16, :] = turned[16 * t : 16 * t + 16, :]
    high = (fy // 256).astype(F32)
    low = (fy % 256).astype(F32)
    tail = jnp.where(iota((8, 128), 0) == 0, high, jnp.where(iota((8, 128), 0) == 1, low, 0.0)).astype(BF16)
    for to in range(32):
        out_ref[to, 64:72, :] = tail


def row_kernel(y_ref, out_ref, tb_ref, acc_ref, e2_ref, e1_ref, fy_ref):
    strip = lax.axis_index("strip")

    def odd_of(shape):
        n = iota(shape, 1)
        return 2 * (32 * ((n % 128) // 16) + 16 * (n // 128) + n % 16) + 1

    e2_t = iota((ROWS, HALF), 0) * odd_of((ROWS, HALF))
    e2_ref[0] = cos_turn(e2_t)
    e2_ref[1] = sin_turn(e2_t)
    for f in range(32):
        tail = y_ref[f, 64:72, :].astype(F32)
        fy_ref[f : f + 1, :] = tail[0:1] * 256.0 + tail[1:2]
    fy = fy_ref[...].astype(jnp.int32)
    fy = jnp.concatenate([fy, fy], axis=1)
    e1_t = (fy + strip * ROWS) * odd_of((32, HALF))
    e1_ref[0] = cos_turn(e1_t)
    e1_ref[1] = sin_turn(e1_t)
    per = BLOCK // 128

    def prepare(b):
        slot = b % 2
        for n in range(per):
            f = b * per + n
            c1 = e1_ref[0, f : f + 1, :]
            s1 = e1_ref[1, f : f + 1, :]
            c2 = e2_ref[0]
            s2 = e2_ref[1]
            tb_ref[slot, n * 128 : n * 128 + 128, :HALF] = (c1 * c2 - s1 * s2).astype(BF16)
            tb_ref[slot, n * 128 : n * 128 + 128, HALF:] = (s1 * c2 + c1 * s2).astype(BF16)

    prepare(0)
    for b in range(BLOCKS):
        if b + 1 < BLOCKS:
            prepare(b + 1)
        left = jnp.concatenate([y_ref[b * per + n, 0:64, :] for n in range(per)], axis=1)
        part = jnp.dot(left, tb_ref[b % 2], preferred_element_type=F32)
        if b == 0:
            acc_ref[...] = part
        else:
            acc_ref[...] += part
    cr = acc_ref[0:32, :HALF]
    sr = acc_ref[0:32, HALF:]
    ci = acc_ref[32:64, :HALF]
    si = acc_ref[32:64, HALF:]
    for sign in (1, -1):
        if sign > 0:
            zr, zi = cr + si, ci - sr
        else:
            zr, zi = cr - si, ci + sr
        z = jnp.concatenate([zr[:, :128], zi[:, :128], zr[:, 128:], zi[:, 128:]], axis=0)
        turned = z.T.astype(out_ref.dtype)
        for t in range(8):
            to = 8 + t if sign > 0 else 7 - t
            out_ref[to] = turned[16 * t : 16 * t + 16, :]


def sum_kernel(z_ref, out_ref):
    strip = lax.axis_index("strip")
    facet = lax.axis_index("facet")
    total = z_ref[0].astype(F32)
    for s in range(1, 16):
        total = total + z_ref[s].astype(F32)
    turn_row = jnp.where(strip < 8, 15, 0)
    turn_lane = jnp.where(strip < 8, 64, 0) + jnp.where(facet < 16, 15, 0)
    left = (iota((16, 16), 1) == (iota((16, 16), 0) ^ turn_row)).astype(F32)
    right = (iota((128, 128), 0) == (iota((128, 128), 1) ^ turn_lane)).astype(F32)
    exact = lax.Precision.HIGHEST
    total = jnp.dot(left, total, precision=exact, preferred_element_type=F32)
    total = jnp.dot(total, right, precision=exact, preferred_element_type=F32)
    for h in range(2):
        for g in range(4):
            at = h * 64 + g * 16
            out_ref[pl.ds(h * 64 + g, 16, stride=4), :] = total[:, at : at + 16]


def vmem():
    return pl.BlockSpec(memory_space=pltpu.VMEM)


def smem():
    return pl.BlockSpec(memory_space=pltpu.SMEM)


def per_device(facet_pixels, facet_offsets, subgrid_offsets):
    limit = pltpu.CompilerParams(vmem_limit_bytes=48 << 20)
    chunks = pl.pallas_call(
        column_kernel,
        out_shape=jax.ShapeDtypeStruct((32, CHUNK_ROWS, 128), BF16),
        in_specs=[pl.BlockSpec(memory_space=pl.ANY), smem(), smem()],
        out_specs=vmem(),
        scratch_shapes=[
            pltpu.VMEM((2, ROWS, WIDTH), BF16),
            pltpu.VMEM((2, 512, BLOCK), BF16),
            pltpu.VMEM((2, BLOCK, 512), BF16),
            pltpu.VMEM((512, 512), F32),
            pltpu.VMEM((2, ROWS, HALF), F32),
            pltpu.VMEM((2, 32, HALF), F32),
            pltpu.VMEM((8, WIDTH), F32),
            pltpu.SemaphoreType.DMA((BLOCKS,)),
        ],
        compiler_params=limit,
        name="column_dft",
    )(facet_pixels, facet_offsets, subgrid_offsets)
    chunks = lax.all_to_all(chunks, "facet", 0, 0, tiled=True)
    parts = pl.pallas_call(
        row_kernel,
        out_shape=jax.ShapeDtypeStruct((16, 16, 128), F32),
        in_specs=[vmem()],
        out_specs=vmem(),
        scratch_shapes=[
            pltpu.VMEM((2, BLOCK, 512), BF16),
            pltpu.VMEM((64, 512), F32),
            pltpu.VMEM((2, ROWS, HALF), F32),
            pltpu.VMEM((2, 32, HALF), F32),
            pltpu.VMEM((32, 128), F32),
        ],
        compiler_params=limit,
        name="row_dft",
    )(chunks)
    parts = lax.all_to_all(parts, "strip", 0, 0, tiled=True)
    out = pl.pallas_call(
        sum_kernel,
        out_shape=jax.ShapeDtypeStruct((128, 16), F32),
        in_specs=[vmem()],
        out_specs=vmem(),
        name="strip_sum",
    )(parts)
    return out.reshape(32, 2, 2, 16)


def solution(mesh):
    in_specs = (P(None, "facet", "strip", None), P("facet", None), P())
    out_specs = P("strip", None, None, "facet")
    return jax.shard_map(
        per_device, mesh=mesh, in_specs=in_specs, out_specs=out_specs, check_vma=False
    )
```

```python
import math

import jax
import jax.numpy as jnp
from jax import lax
from jax.experimental import pallas as pl
from jax.experimental.pallas import tpu as pltpu
from jax.sharding import PartitionSpec as P

TURN = 131072
HALF = 256
FREQ = 512
COLUMNS = 2
ROWS = 128
WIDTH = 4096
BLOCKS = 8
BLOCK = WIDTH // BLOCKS
CHUNK_ROWS = 72
F32 = jnp.float32
BF16 = jnp.bfloat16


def cos_turn(t):
    v = jnp.abs((t & (TURN - 1)) - TURN // 2) - TURN // 4
    z = v.astype(F32) * (2.0 * math.pi / TURN)
    q = z * z
    p = -1.0 / 39916800.0
    for term in (1.0 / 362880.0, -1.0 / 5040.0, 1.0 / 120.0, -1.0 / 6.0):
        p = p * q + term
    return z + z * (q * p)


def sin_turn(t):
    return cos_turn(t - TURN // 4)


def iota(shape, axis):
    return lax.broadcasted_iota(jnp.int32, shape, axis)


def fill_low_table(e2_ref, odd):
    q_t = iota((8, HALF), 0) * odd
    p_t = iota((16, HALF), 0) * (8 * odd[0:1])
    qc, qs, pc, ps = cos_turn(q_t), sin_turn(q_t), cos_turn(p_t), sin_turn(p_t)
    for p in range(16):
        c1, s1 = pc[p : p + 1], ps[p : p + 1]
        e2_ref[0, 8 * p : 8 * p + 8, :] = c1 * qc - s1 * qs
        e2_ref[1, 8 * p : 8 * p + 8, :] = s1 * qc + c1 * qs


def fill_block(tb_ref, slot, n, e1_ref, at, e2_ref):
    c1 = e1_ref[0, at : at + 1, :]
    s1 = e1_ref[1, at : at + 1, :]
    c2 = e2_ref[0]
    s2 = e2_ref[1]
    tb_ref[slot, n * 128 : n * 128 + 128, :HALF] = (c1 * c2 - s1 * s2).astype(BF16)
    tb_ref[slot, n * 128 : n * 128 + 128, HALF:] = (s1 * c2 + c1 * s2).astype(BF16)


def mirror():
    return (iota((HALF, HALF), 0) + iota((HALF, HALF), 1) == HALF - 1).astype(BF16)


def column_kernel(
    x_hbm, facet_hbm, sub_hbm, out_ref, x_ref, facet_ref, sub_ref, xp_ref, tb_ref, acc_ref, e2_ref, e1_ref, tw_ref, sems
):
    small = [
        pltpu.make_async_copy(facet_hbm, facet_ref, sems.at[BLOCKS]),
        pltpu.make_async_copy(sub_hbm, sub_ref, sems.at[BLOCKS + 1]),
    ]
    copies = [
        pltpu.make_async_copy(
            x_hbm.at[:, 0, :, pl.ds(b * BLOCK, BLOCK)],
            x_ref.at[:, :, pl.ds(b * BLOCK, BLOCK)],
            sems.at[b],
        )
        for b in range(BLOCKS)
    ]
    for copy in small + copies:
        copy.start()
    strip = lax.axis_index("strip")
    odd = 2 * iota((8, HALF), 1) + 1
    fill_low_table(e2_ref, odd)
    e1_t = iota((32, HALF), 0) * (128 * (2 * iota((32, HALF), 1) + 1))
    e1_ref[0] = cos_turn(e1_t)
    e1_ref[1] = sin_turn(e1_t)
    for copy in small:
        copy.wait()
    fx = facet_ref[0, 0]
    fy = facet_ref[0, 1]
    row = iota((8, WIDTH // 2), 0)
    centre = jnp.where(row % 2 == 0, 2 * sub_ref[0, 0] + 511, 2 * sub_ref[1, 0] + 511)
    pixel = iota((8, WIDTH // 2), 1) + jnp.where(row >= 4, WIDTH // 2, 0)
    tw_ref[...] = cos_turn(pixel * centre - jnp.where(row % 4 >= 2, TURN // 4, 0))

    def prepare(b, tiles):
        if 0 in tiles:
            copies[b].wait()
        slot = b % 2
        for n in tiles:
            lo = b * BLOCK + n * 128
            half, at = 4 * (lo // (WIDTH // 2)), lo % (WIDTH // 2)
            xr = x_ref[0, :, lo : lo + 128].astype(F32)
            xi = x_ref[1, :, lo : lo + 128].astype(F32)
            for c in range(COLUMNS):
                wc = tw_ref[half + c : half + c + 1, at : at + 128]
                ws = tw_ref[half + 2 + c : half + 3 + c, at : at + 128]
                base = c * 2 * ROWS
                xp_ref[slot, base : base + ROWS, n * 128 : n * 128 + 128] = (xr * wc + xi * ws).astype(BF16)
                xp_ref[slot, base + ROWS : base + 2 * ROWS, n * 128 : n * 128 + 128] = (xi * wc - xr * ws).astype(BF16)
            fill_block(tb_ref, slot, n, e1_ref, lo // 128, e2_ref)

    tiles = BLOCK // 128
    prepare(0, range(tiles))
    for b in range(BLOCKS):
        for h in range(2):
            if b + 1 < BLOCKS:
                prepare(b + 1, range(h * tiles // 2, (h + 1) * tiles // 2))
            cols = slice(h * HALF, h * HALF + HALF)
            part = jnp.dot(xp_ref[b % 2], tb_ref[b % 2, :, cols], preferred_element_type=F32)
            if b == 0:
                acc_ref[:, cols] = part
            else:
                acc_ref[:, cols] += part

    psi_t = fx * odd
    cpsi = cos_turn(psi_t)[0:1]
    spsi = sin_turn(psi_t)[0:1]
    turn = mirror()
    scale = 1.0 / 16384.0
    for c in range(COLUMNS):
        step = 2 * sub_ref[c, 1] + 511
        q_t = (fy + strip * ROWS + iota((8, 128), 0)) * step + fx * (2 * sub_ref[c, 0] + 511)
        p_t = iota((16, 128), 0) * (8 * step)
        qc, qs, pc, ps = cos_turn(q_t) * scale, sin_turn(q_t) * scale, cos_turn(p_t), sin_turn(p_t)
        cphi = jnp.concatenate([pc[p : p + 1] * qc - ps[p : p + 1] * qs for p in range(16)], axis=0)
        sphi = jnp.concatenate([ps[p : p + 1] * qc + pc[p : p + 1] * qs for p in range(16)], axis=0)
        base = c * 2 * ROWS
        plus, minus = [[], []], [[], []]
        for lo in range(0, HALF, 128):
            cp, sp = cpsi[:, lo : lo + 128], spsi[:, lo : lo + 128]
            cr = acc_ref[base : base + ROWS, lo : lo + 128]
            sr = acc_ref[base : base + ROWS, HALF + lo : HALF + lo + 128]
            ci = acc_ref[base + ROWS : base + 2 * ROWS, lo : lo + 128]
            si = acc_ref[base + ROWS : base + 2 * ROWS, HALF + lo : HALF + lo + 128]
            cc, ss, sc, cs = cphi * cp, sphi * sp, sphi * cp, cphi * sp
            yr, yi, pc, ps = cr + si, ci - sr, cc - ss, sc + cs
            plus[0].append(yr * pc + yi * ps)
            plus[1].append(yi * pc - yr * ps)
            yr, yi, pc, ps = cr - si, ci + sr, cc + ss, sc - cs
            minus[0].append((yr * pc + yi * ps).astype(BF16))
            minus[1].append((yi * pc - yr * ps).astype(BF16))
        for part in range(2):
            at = (part * 2 + c) * 16
            for h in range(2):
                turned = plus[part][h].T.astype(BF16)
                for t in range(8):
                    out_ref[16 + 8 * h + t, at : at + 16, :] = turned[16 * t : 16 * t + 16, :]
            turned = lax.dot_general(
                turn, jnp.concatenate(minus[part], axis=1), (((1,), (1,)), ((), ())), preferred_element_type=F32
            ).astype(BF16)
            for t in range(16):
                out_ref[t, at : at + 16, :] = turned[16 * t : 16 * t + 16, :]
    high = (fy // 256).astype(F32)
    low = (fy % 256).astype(F32)
    tail = jnp.where(iota((8, 128), 0) == 0, high, jnp.where(iota((8, 128), 0) == 1, low, 0.0)).astype(BF16)
    for to in range(32):
        out_ref[to, 64:72, :] = tail


def row_kernel(y_ref, out_ref, tb_ref, acc_ref, e2_ref, e1_ref, fy_ref):
    strip = lax.axis_index("strip")

    def odd_of(rows):
        n = iota((rows, HALF), 1)
        return 2 * (32 * ((n % 128) // 16) + 16 * (n // 128) + n % 16) + 1

    fill_low_table(e2_ref, odd_of(8))
    for f in range(32):
        tail = y_ref[f, 64:72, :].astype(F32)
        fy_ref[f : f + 1, :] = tail[0:1] * 256.0 + tail[1:2]
    fy = fy_ref[...].astype(jnp.int32)
    fy = jnp.concatenate([fy, fy], axis=1)
    e1_t = (fy + strip * ROWS) * odd_of(32)
    e1_ref[0] = cos_turn(e1_t)
    e1_ref[1] = sin_turn(e1_t)
    per = BLOCK // 128

    def prepare(b):
        for n in range(per):
            fill_block(tb_ref, b % 2, n, e1_ref, b * per + n, e2_ref)

    prepare(0)
    for b in range(BLOCKS):
        if b + 1 < BLOCKS:
            prepare(b + 1)
        left = jnp.concatenate([y_ref[b * per + n, 0:64, :] for n in range(per)], axis=1)
        part = jnp.dot(left, tb_ref[b % 2], preferred_element_type=F32)
        if b == 0:
            acc_ref[...] = part
        else:
            acc_ref[...] += part
    cr = acc_ref[0:32, :HALF]
    sr = acc_ref[0:32, HALF:]
    ci = acc_ref[32:64, :HALF]
    si = acc_ref[32:64, HALF:]
    plus = jnp.concatenate([cr + si, ci - sr], axis=0)
    minus = jnp.concatenate([cr - si, ci + sr], axis=0).astype(BF16)
    minus = jnp.dot(minus, mirror(), preferred_element_type=F32)
    for first, z in ((8, plus), (0, minus)):
        turned = jnp.concatenate([z[:, :128], z[:, 128:]], axis=0).T.astype(BF16)
        for t in range(8):
            out_ref[first + t] = turned[16 * t : 16 * t + 16, :]


def sum_kernel(z_ref, out_ref):
    parts = [z_ref[s].astype(F32) for s in range(16)]
    while len(parts) > 1:
        parts = [a + b for a, b in zip(parts[::2], parts[1::2], strict=True)]
    turned = parts[0].T
    out_ref[:, 0:16] = turned[0:64]
    out_ref[:, 16:32] = turned[64:128]


def vmem():
    return pl.BlockSpec(memory_space=pltpu.VMEM)


def hbm():
    return pl.BlockSpec(memory_space=pltpu.HBM)


def per_device(facet_pixels, facet_offsets, subgrid_offsets):
    limit = pltpu.CompilerParams(vmem_limit_bytes=48 << 20)
    chunks = pl.pallas_call(
        column_kernel,
        out_shape=jax.ShapeDtypeStruct((32, CHUNK_ROWS, 128), BF16),
        in_specs=[hbm(), hbm(), hbm()],
        out_specs=vmem(),
        scratch_shapes=[
            pltpu.VMEM((2, ROWS, WIDTH), BF16),
            pltpu.SMEM((1, 2), jnp.int32),
            pltpu.SMEM((2, 2), jnp.int32),
            pltpu.VMEM((2, 512, BLOCK), BF16),
            pltpu.VMEM((2, BLOCK, 512), BF16),
            pltpu.VMEM((512, 512), F32),
            pltpu.VMEM((2, ROWS, HALF), F32),
            pltpu.VMEM((2, 32, HALF), F32),
            pltpu.VMEM((8, WIDTH // 2), F32),
            pltpu.SemaphoreType.DMA((BLOCKS + 2,)),
        ],
        compiler_params=limit,
        name="column_dft",
    )(*(pltpu.with_memory_space_constraint(a, pltpu.HBM) for a in (facet_pixels, facet_offsets, subgrid_offsets)))
    chunks = lax.all_to_all(chunks, "facet", 0, 0, tiled=True)
    parts = pl.pallas_call(
        row_kernel,
        out_shape=jax.ShapeDtypeStruct((16, 16, 128), BF16),
        in_specs=[vmem()],
        out_specs=vmem(),
        scratch_shapes=[
            pltpu.VMEM((2, BLOCK, 512), BF16),
            pltpu.VMEM((64, 512), F32),
            pltpu.VMEM((2, ROWS, HALF), F32),
            pltpu.VMEM((2, 32, HALF), F32),
            pltpu.VMEM((32, 128), F32),
        ],
        compiler_params=limit,
        name="row_dft",
    )(chunks)
    parts = lax.all_to_all(parts, "strip", 0, 0, tiled=True)
    out = pl.pallas_call(
        sum_kernel,
        out_shape=jax.ShapeDtypeStruct((64, 32), F32),
        in_specs=[vmem()],
        out_specs=vmem(),
        name="strip_sum",
    )(parts)
    return jnp.transpose(out.reshape(2, 2, 16, 32), (3, 0, 1, 2))


def solution(mesh):
    in_specs = (P(None, "facet", "strip", None), P("facet", None), P())
    out_specs = P("strip", None, None, "facet")
    return jax.shard_map(
        per_device, mesh=mesh, in_specs=in_specs, out_specs=out_specs, check_vma=False
    )
```

```python
import math

import jax
import jax.numpy as jnp
from jax import lax
from jax.experimental import pallas as pl
from jax.experimental.pallas import tpu as pltpu
from jax.sharding import PartitionSpec as P

TURN = 262144
HALF = 256
FREQ = 512
COLUMNS = 2
ROWS = 128
WIDTH = 4096
MIDDLE = WIDTH // 2
BLOCK = 512
BLOCKS = MIDDLE // BLOCK
ROW_BLOCK = 512
ROW_BLOCKS = 32 * ROWS // ROW_BLOCK
CHUNK_ROWS = 72
STEP = 16
XSTEP = 32
F32 = jnp.float32
BF16 = jnp.bfloat16


def cos_turn(t):
    v = jnp.abs((t & (TURN - 1)) - TURN // 2) - TURN // 4
    z = v.astype(F32) * (2.0 * math.pi / TURN)
    q = z * z
    p = -1.0 / 39916800.0
    for term in (1.0 / 362880.0, -1.0 / 5040.0, 1.0 / 120.0, -1.0 / 6.0):
        p = p * q + term
    return z + z * (q * p)


def sin_turn(t):
    return cos_turn(t - TURN // 4)


def iota(shape, axis):
    return lax.broadcasted_iota(jnp.int32, shape, axis)


def fill_low_table(e2_ref, odd, first):
    q_t = (2 * iota((8, HALF), 0) + first) * odd
    p_t = iota((16, HALF), 0) * (16 * odd[0:1])
    qc, qs, pc, ps = cos_turn(q_t), sin_turn(q_t), cos_turn(p_t), sin_turn(p_t)
    for p in range(16):
        c1, s1 = pc[p : p + 1], ps[p : p + 1]
        e2_ref[0, 8 * p : 8 * p + 8, :] = c1 * qc - s1 * qs
        e2_ref[1, 8 * p : 8 * p + 8, :] = s1 * qc + c1 * qs


def fill_block(tb_ref, slot, n, e1_ref, at, e2_ref):
    c1 = e1_ref[0, at : at + 1, :]
    s1 = e1_ref[1, at : at + 1, :]
    for r in range(0, ROWS, STEP):
        c2 = e2_ref[0, r : r + STEP, :]
        s2 = e2_ref[1, r : r + STEP, :]
        to = slice(n * 128 + r, n * 128 + r + STEP)
        tb_ref[slot, to, :HALF] = (c1 * c2 - s1 * s2).astype(BF16)
        tb_ref[slot, to, HALF:] = (s1 * c2 + c1 * s2).astype(BF16)


def mirror():
    return (iota((HALF, HALF), 0) + iota((HALF, HALF), 1) == HALF - 1).astype(BF16)


def column_kernel(
    x_hbm, facet_hbm, sub_hbm, out_ref, x_ref, facet_ref, sub_ref, xp_ref, tb_ref, acc_ref, e2_ref, e1_ref, tw_ref, sems
):
    small = [
        pltpu.make_async_copy(facet_hbm, facet_ref, sems.at[2 * BLOCKS]),
        pltpu.make_async_copy(sub_hbm, sub_ref, sems.at[2 * BLOCKS + 1]),
    ]
    copies = []
    for b in range(BLOCKS):
        for side, lo in enumerate((MIDDLE + b * BLOCK, MIDDLE - (b + 1) * BLOCK)):
            span = pl.ds(lo, BLOCK)
            copies.append(
                pltpu.make_async_copy(x_hbm.at[:, 0, :, span], x_ref.at[:, :, span], sems.at[2 * b + side])
            )
    for copy in small + copies:
        copy.start()
    strip = lax.axis_index("strip")
    odd = 2 * iota((8, HALF), 1) + 1
    fill_low_table(e2_ref, odd, 1)
    e1_t = iota((16, HALF), 0) * (256 * (2 * iota((16, HALF), 1) + 1))
    e1_ref[0] = cos_turn(e1_t)
    e1_ref[1] = sin_turn(e1_t)
    for copy in small:
        copy.wait()
    fx = facet_ref[0, 0]
    fy = facet_ref[0, 1]
    row = iota((8, MIDDLE // 2), 0)
    centre = jnp.where(row % 2 == 0, 2 * sub_ref[0, 0] + 511, 2 * sub_ref[1, 0] + 511)
    odd_pixel = 2 * (iota((8, MIDDLE // 2), 1) + jnp.where(row >= 4, MIDDLE // 2, 0)) + 1
    tw_ref[...] = cos_turn(odd_pixel * centre - jnp.where(row % 4 >= 2, TURN // 4, 0))
    turn = mirror()

    def prepare(b, pairs):
        if 0 in pairs:
            copies[2 * b].wait()
            copies[2 * b + 1].wait()
        slot = b % 2
        for pair in pairs:
            low = MIDDLE - b * BLOCK - 256 * (pair + 1)
            turned = [
                jnp.dot(x_ref[part, :, low : low + 256], turn, preferred_element_type=F32) for part in range(2)
            ]
            for n in range(2 * pair, 2 * pair + 2):
                lo = b * BLOCK + n * 128
                half, at = 4 * (lo // (MIDDLE // 2)), lo % (MIDDLE // 2)
                to = slice(n * 128, n * 128 + 128)
                side = slice(128 * (n % 2), 128 * (n % 2) + 128)
                turns = [
                    [tw_ref[half + q + c : half + q + c + 1, at : at + 128] for q in (0, 2)] for c in range(COLUMNS)
                ]
                for r in range(0, ROWS, XSTEP):
                    up = slice(MIDDLE + lo, MIDDLE + lo + 128)
                    ar = x_ref[0, r : r + XSTEP, up].astype(F32)
                    ai = x_ref[1, r : r + XSTEP, up].astype(F32)
                    br = turned[0][r : r + XSTEP, side]
                    bi = turned[1][r : r + XSTEP, side]
                    pr, pi, qr, qi = ar + br, ai + bi, ar - br, ai - bi
                    for c, (wc, ws) in enumerate(turns):
                        row = c * 2 * ROWS + r
                        xp_ref[slot, 0, row : row + XSTEP, to] = (pr * wc + qi * ws).astype(BF16)
                        xp_ref[slot, 1, row : row + XSTEP, to] = (qr * wc + pi * ws).astype(BF16)
                        row += ROWS
                        xp_ref[slot, 0, row : row + XSTEP, to] = (pi * wc - qr * ws).astype(BF16)
                        xp_ref[slot, 1, row : row + XSTEP, to] = (qi * wc - pr * ws).astype(BF16)
                fill_block(tb_ref, slot, n, e1_ref, lo // 128, e2_ref)

    pairs = BLOCK // 256
    prepare(0, range(pairs))
    for b in range(BLOCKS):
        for h in range(2):
            if b + 1 < BLOCKS:
                prepare(b + 1, range(h * pairs // 2, (h + 1) * pairs // 2))
            cols = slice(h * HALF, h * HALF + HALF)
            part = jnp.dot(xp_ref[b % 2, h], tb_ref[b % 2, :, cols], preferred_element_type=F32)
            if b == 0:
                acc_ref[:, cols] = part
            else:
                acc_ref[:, cols] += part

    psi_t = (2 * fx + WIDTH - 1) * odd
    cpsi = cos_turn(psi_t)[0:1]
    spsi = sin_turn(psi_t)[0:1]
    scale = 1.0 / 16384.0
    for c in range(COLUMNS):
        step = 2 * (2 * sub_ref[c, 1] + 511)
        q_t = (fy + strip * ROWS + iota((8, 128), 0)) * step + (2 * fx + WIDTH - 1) * (
            2 * sub_ref[c, 0] + 511
        )
        p_t = iota((16, 128), 0) * (8 * step)
        qc, qs, pc, ps = cos_turn(q_t) * scale, sin_turn(q_t) * scale, cos_turn(p_t), sin_turn(p_t)
        cphi = jnp.concatenate([pc[p : p + 1] * qc - ps[p : p + 1] * qs for p in range(16)], axis=0)
        sphi = jnp.concatenate([ps[p : p + 1] * qc + pc[p : p + 1] * qs for p in range(16)], axis=0)
        base = c * 2 * ROWS
        plus, minus = [[], []], [[], []]
        for lo in range(0, HALF, 128):
            cp, sp = cpsi[:, lo : lo + 128], spsi[:, lo : lo + 128]
            cr = acc_ref[base : base + ROWS, lo : lo + 128]
            sr = acc_ref[base : base + ROWS, HALF + lo : HALF + lo + 128]
            ci = acc_ref[base + ROWS : base + 2 * ROWS, lo : lo + 128]
            si = acc_ref[base + ROWS : base + 2 * ROWS, HALF + lo : HALF + lo + 128]
            cc, ss, sc, cs = cphi * cp, sphi * sp, sphi * cp, cphi * sp
            yr, yi, pc, ps = cr + si, ci - sr, cc - ss, sc + cs
            plus[0].append(yr * pc + yi * ps)
            plus[1].append(yi * pc - yr * ps)
            yr, yi, pc, ps = cr - si, ci + sr, cc + ss, sc - cs
            minus[0].append((yr * pc + yi * ps).astype(BF16))
            minus[1].append((yi * pc - yr * ps).astype(BF16))
        for part in range(2):
            at = (part * 2 + c) * 16
            for h in range(2):
                turned = plus[part][h].T.astype(BF16)
                for t in range(8):
                    out_ref[16 + 8 * h + t, at : at + 16, :] = turned[16 * t : 16 * t + 16, :]
            turned = lax.dot_general(
                turn, jnp.concatenate(minus[part], axis=1), (((1,), (1,)), ((), ())), preferred_element_type=F32
            ).astype(BF16)
            for t in range(16):
                out_ref[t, at : at + 16, :] = turned[16 * t : 16 * t + 16, :]
    high = (fy // 256).astype(F32)
    low = (fy % 256).astype(F32)
    tail = jnp.where(iota((8, 128), 0) == 0, high, jnp.where(iota((8, 128), 0) == 1, low, 0.0)).astype(BF16)
    for to in range(32):
        out_ref[to, 64:72, :] = tail


def row_kernel(y_ref, out_ref, tb_ref, acc_ref, e2_ref, e1_ref, fy_ref):
    strip = lax.axis_index("strip")

    def odd_of(rows):
        n = iota((rows, HALF), 1)
        return 2 * (32 * ((n % 128) // 16) + 16 * (n // 128) + n % 16) + 1

    fill_low_table(e2_ref, odd_of(8), 0)
    for f in range(32):
        tail = y_ref[f, 64:72, :].astype(F32)
        fy_ref[f : f + 1, :] = tail[0:1] * 256.0 + tail[1:2]
    fy = fy_ref[...].astype(jnp.int32)
    fy = jnp.concatenate([fy, fy], axis=1)
    e1_t = 2 * (fy + strip * ROWS) * odd_of(32)
    e1_ref[0] = cos_turn(e1_t)
    e1_ref[1] = sin_turn(e1_t)
    per = ROW_BLOCK // 128

    def prepare(b):
        for n in range(per):
            fill_block(tb_ref, b % 2, n, e1_ref, b * per + n, e2_ref)

    prepare(0)
    for b in range(ROW_BLOCKS):
        if b + 1 < ROW_BLOCKS:
            prepare(b + 1)
        left = jnp.concatenate([y_ref[b * per + n, 0:64, :] for n in range(per)], axis=1)
        part = jnp.dot(left, tb_ref[b % 2], preferred_element_type=F32)
        if b == 0:
            acc_ref[...] = part
        else:
            acc_ref[...] += part
    cr = acc_ref[0:32, :HALF]
    sr = acc_ref[0:32, HALF:]
    ci = acc_ref[32:64, :HALF]
    si = acc_ref[32:64, HALF:]
    plus = jnp.concatenate([cr + si, ci - sr], axis=0)
    minus = jnp.concatenate([cr - si, ci + sr], axis=0).astype(BF16)
    minus = jnp.dot(minus, mirror(), preferred_element_type=F32)
    for first, z in ((8, plus), (0, minus)):
        turned = jnp.concatenate([z[:, :128], z[:, 128:]], axis=0).T.astype(BF16)
        for t in range(8):
            out_ref[first + t] = turned[16 * t : 16 * t + 16, :]


def sum_kernel(z_ref, out_ref):
    parts = [z_ref[s].astype(F32) for s in range(16)]
    while len(parts) > 1:
        parts = [a + b for a, b in zip(parts[::2], parts[1::2], strict=True)]
    turned = parts[0].T
    out_ref[:, 0:16] = turned[0:64]
    out_ref[:, 16:32] = turned[64:128]


def vmem():
    return pl.BlockSpec(memory_space=pltpu.VMEM)


def hbm():
    return pl.BlockSpec(memory_space=pltpu.HBM)


def per_device(facet_pixels, facet_offsets, subgrid_offsets):
    limit = pltpu.CompilerParams(vmem_limit_bytes=48 << 20)
    chunks = pl.pallas_call(
        column_kernel,
        out_shape=jax.ShapeDtypeStruct((32, CHUNK_ROWS, 128), BF16),
        in_specs=[hbm(), hbm(), hbm()],
        out_specs=vmem(),
        scratch_shapes=[
            pltpu.VMEM((2, ROWS, WIDTH), BF16),
            pltpu.SMEM((1, 2), jnp.int32),
            pltpu.SMEM((2, 2), jnp.int32),
            pltpu.VMEM((2, 2, 512, BLOCK), BF16),
            pltpu.VMEM((2, BLOCK, 512), BF16),
            pltpu.VMEM((512, 512), F32),
            pltpu.VMEM((2, ROWS, HALF), F32),
            pltpu.VMEM((2, 16, HALF), F32),
            pltpu.VMEM((8, MIDDLE // 2), F32),
            pltpu.SemaphoreType.DMA((2 * BLOCKS + 2,)),
        ],
        compiler_params=limit,
        name="column_dft",
    )(*(pltpu.with_memory_space_constraint(a, pltpu.HBM) for a in (facet_pixels, facet_offsets, subgrid_offsets)))
    chunks = lax.all_to_all(chunks, "facet", 0, 0, tiled=True)
    parts = pl.pallas_call(
        row_kernel,
        out_shape=jax.ShapeDtypeStruct((16, 16, 128), BF16),
        in_specs=[vmem()],
        out_specs=vmem(),
        scratch_shapes=[
            pltpu.VMEM((2, ROW_BLOCK, 512), BF16),
            pltpu.VMEM((64, 512), F32),
            pltpu.VMEM((2, ROWS, HALF), F32),
            pltpu.VMEM((2, 32, HALF), F32),
            pltpu.VMEM((32, 128), F32),
        ],
        compiler_params=limit,
        name="row_dft",
    )(chunks)
    parts = lax.all_to_all(parts, "strip", 0, 0, tiled=True)
    out = pl.pallas_call(
        sum_kernel,
        out_shape=jax.ShapeDtypeStruct((64, 32), F32),
        in_specs=[vmem()],
        out_specs=vmem(),
        name="strip_sum",
    )(pltpu.with_memory_space_constraint(parts, pltpu.VMEM))
    return jnp.transpose(out.reshape(2, 2, 16, 32), (3, 0, 1, 2))


def solution(mesh):
    in_specs = (P(None, "facet", "strip", None), P("facet", None), P())
    out_specs = P("strip", None, None, "facet")
    return jax.shard_map(
        per_device, mesh=mesh, in_specs=in_specs, out_specs=out_specs, check_vma=False
    )
```

```python
import math

import jax
import jax.numpy as jnp
from jax import lax
from jax.experimental import pallas as pl
from jax.experimental.pallas import tpu as pltpu
from jax.sharding import PartitionSpec as P

TURN = 262144
HALF = 256
FREQ = 512
COLUMNS = 2
ROWS = 128
WIDTH = 4096
MIDDLE = WIDTH // 2
BLOCK = 512
BLOCKS = MIDDLE // BLOCK
ROW_BLOCK = 512
ROW_BLOCKS = 32 * ROWS // ROW_BLOCK
CHUNK_ROWS = 72
STEP = 16
XSTEP = 32
F32 = jnp.float32
BF16 = jnp.bfloat16


def cos_turn(t):
    v = jnp.abs((t & (TURN - 1)) - TURN // 2) - TURN // 4
    z = v.astype(F32) * (2.0 * math.pi / TURN)
    q = z * z
    p = -1.0 / 39916800.0
    for term in (1.0 / 362880.0, -1.0 / 5040.0, 1.0 / 120.0, -1.0 / 6.0):
        p = p * q + term
    return z + z * (q * p)


def sin_turn(t):
    return cos_turn(t - TURN // 4)


def iota(shape, axis):
    return lax.broadcasted_iota(jnp.int32, shape, axis)


def fill_low_table(e2_ref, odd):
    q_t = (2 * iota((8, HALF), 0) + 1) * odd
    p_t = iota((16, HALF), 0) * (16 * odd[0:1])
    qc, qs, pc, ps = cos_turn(q_t), sin_turn(q_t), cos_turn(p_t), sin_turn(p_t)
    for p in range(e2_ref.shape[1] // 8):
        c1, s1 = pc[p : p + 1], ps[p : p + 1]
        e2_ref[0, 8 * p : 8 * p + 8, :] = c1 * qc - s1 * qs
        e2_ref[1, 8 * p : 8 * p + 8, :] = s1 * qc + c1 * qs


def fill_block(tb_ref, slot, n, e1_ref, at, e2_ref):
    c1 = e1_ref[0, at : at + 1, :]
    s1 = e1_ref[1, at : at + 1, :]
    for r in range(0, ROWS, STEP):
        c2 = e2_ref[0, r : r + STEP, :]
        s2 = e2_ref[1, r : r + STEP, :]
        to = slice(n * 128 + r, n * 128 + r + STEP)
        tb_ref[slot, to, :HALF] = (c1 * c2 - s1 * s2).astype(BF16)
        tb_ref[slot, to, HALF:] = (s1 * c2 + c1 * s2).astype(BF16)


def mirror():
    return (iota((HALF, HALF), 0) + iota((HALF, HALF), 1) == HALF - 1).astype(BF16)


def column_kernel(
    x_hbm, facet_hbm, sub_hbm, out_ref, x_ref, facet_ref, sub_ref, xp_ref, tb_ref, acc_ref, e2_ref, e1_ref, tw_ref, sems
):
    small = [
        pltpu.make_async_copy(facet_hbm, facet_ref, sems.at[2 * BLOCKS]),
        pltpu.make_async_copy(sub_hbm, sub_ref, sems.at[2 * BLOCKS + 1]),
    ]
    copies = []
    for b in range(BLOCKS):
        for side, lo in enumerate((MIDDLE + b * BLOCK, MIDDLE - (b + 1) * BLOCK)):
            span = pl.ds(lo, BLOCK)
            copies.append(
                pltpu.make_async_copy(x_hbm.at[:, 0, :, span], x_ref.at[:, :, span], sems.at[2 * b + side])
            )
    for copy in small + copies:
        copy.start()
    strip = lax.axis_index("strip")
    odd = 2 * iota((8, HALF), 1) + 1
    fill_low_table(e2_ref, odd)
    e1_t = iota((16, HALF), 0) * (256 * (2 * iota((16, HALF), 1) + 1))
    e1_ref[0] = cos_turn(e1_t)
    e1_ref[1] = sin_turn(e1_t)
    for copy in small:
        copy.wait()
    fx = facet_ref[0, 0]
    fy = facet_ref[0, 1]
    row = iota((8, MIDDLE // 2), 0)
    centre = jnp.where(row % 2 == 0, 2 * sub_ref[0, 0] + 511, 2 * sub_ref[1, 0] + 511)
    odd_pixel = 2 * (iota((8, MIDDLE // 2), 1) + jnp.where(row >= 4, MIDDLE // 2, 0)) + 1
    tw_ref[...] = cos_turn(odd_pixel * centre - jnp.where(row % 4 >= 2, TURN // 4, 0))
    turn = mirror()

    def prepare(b, pairs):
        if 0 in pairs:
            copies[2 * b].wait()
            copies[2 * b + 1].wait()
        slot = b % 2
        for pair in pairs:
            low = MIDDLE - b * BLOCK - 256 * (pair + 1)
            turned = [
                jnp.dot(x_ref[part, :, low : low + 256], turn, preferred_element_type=F32) for part in range(2)
            ]
            for n in range(2 * pair, 2 * pair + 2):
                lo = b * BLOCK + n * 128
                half, at = 4 * (lo // (MIDDLE // 2)), lo % (MIDDLE // 2)
                to = slice(n * 128, n * 128 + 128)
                side = slice(128 * (n % 2), 128 * (n % 2) + 128)
                turns = [
                    [tw_ref[half + q + c : half + q + c + 1, at : at + 128] for q in (0, 2)] for c in range(COLUMNS)
                ]
                for r in range(0, ROWS, XSTEP):
                    up = slice(MIDDLE + lo, MIDDLE + lo + 128)
                    ar = x_ref[0, r : r + XSTEP, up].astype(F32)
                    ai = x_ref[1, r : r + XSTEP, up].astype(F32)
                    br = turned[0][r : r + XSTEP, side]
                    bi = turned[1][r : r + XSTEP, side]
                    pr, pi, qr, qi = ar + br, ai + bi, ar - br, ai - bi
                    for c, (wc, ws) in enumerate(turns):
                        row = c * 2 * ROWS + r
                        xp_ref[slot, 0, row : row + XSTEP, to] = (pr * wc + qi * ws).astype(BF16)
                        xp_ref[slot, 1, row : row + XSTEP, to] = (qr * wc + pi * ws).astype(BF16)
                        row += ROWS
                        xp_ref[slot, 0, row : row + XSTEP, to] = (pi * wc - qr * ws).astype(BF16)
                        xp_ref[slot, 1, row : row + XSTEP, to] = (qi * wc - pr * ws).astype(BF16)
                fill_block(tb_ref, slot, n, e1_ref, lo // 128, e2_ref)

    pairs = BLOCK // 256
    prepare(0, range(pairs))
    for b in range(BLOCKS):
        for h in range(2):
            if b + 1 < BLOCKS:
                prepare(b + 1, range(h * pairs // 2, (h + 1) * pairs // 2))
            cols = slice(h * HALF, h * HALF + HALF)
            part = jnp.dot(xp_ref[b % 2, h], tb_ref[b % 2, :, cols], preferred_element_type=F32)
            if b == 0:
                acc_ref[:, cols] = part
            else:
                acc_ref[:, cols] += part

    to, at = iota((ROWS, ROWS), 0), iota((ROWS, ROWS), 1)
    lower = (at == 63 - to % 64).astype(F32)
    fold = ((at == 64 + to % 64).astype(F32) + jnp.where(to < 64, lower, -lower)).astype(BF16)
    psi_t = (2 * fx + WIDTH - 1) * odd
    cpsi = cos_turn(psi_t)[0:1]
    spsi = sin_turn(psi_t)[0:1]
    scale = 1.0 / 16384.0
    places, pluses, minuses = [], [], []
    for c in range(COLUMNS):
        step = 2 * (2 * sub_ref[c, 1] + 511)
        q_t = (fy + strip * ROWS + iota((8, 128), 0)) * step + (2 * fx + WIDTH - 1) * (
            2 * sub_ref[c, 0] + 511
        )
        p_t = iota((16, 128), 0) * (8 * step)
        qc, qs, pc, ps = cos_turn(q_t) * scale, sin_turn(q_t) * scale, cos_turn(p_t), sin_turn(p_t)
        cphi = jnp.concatenate([pc[p : p + 1] * qc - ps[p : p + 1] * qs for p in range(16)], axis=0)
        sphi = jnp.concatenate([ps[p : p + 1] * qc + pc[p : p + 1] * qs for p in range(16)], axis=0)
        base = c * 2 * ROWS
        plus, minus = [[], []], [[], []]
        for lo in range(0, HALF, 128):
            cp, sp = cpsi[:, lo : lo + 128], spsi[:, lo : lo + 128]
            cr = acc_ref[base : base + ROWS, lo : lo + 128]
            sr = acc_ref[base : base + ROWS, HALF + lo : HALF + lo + 128]
            ci = acc_ref[base + ROWS : base + 2 * ROWS, lo : lo + 128]
            si = acc_ref[base + ROWS : base + 2 * ROWS, HALF + lo : HALF + lo + 128]
            cc, ss, sc, cs = cphi * cp, sphi * sp, sphi * cp, cphi * sp
            yr, yi, pc, ps = cr + si, ci - sr, cc - ss, sc + cs
            plus[0].append((yr * pc + yi * ps).astype(BF16))
            plus[1].append((yi * pc - yr * ps).astype(BF16))
            yr, yi, pc, ps = cr - si, ci + sr, cc + ss, sc - cs
            minus[0].append((yr * pc + yi * ps).astype(BF16))
            minus[1].append((yi * pc - yr * ps).astype(BF16))
        for part in range(2):
            places.append((part * 2 + c) * 16)
            pluses.append(jnp.concatenate(plus[part], axis=1))
            minuses.append(jnp.concatenate(minus[part], axis=1))
    folded = jnp.dot(fold, jnp.concatenate(pluses, axis=1), preferred_element_type=F32)
    for n, at in enumerate(places):
        for h in range(2):
            turned = folded[:, n * HALF + h * 128 : n * HALF + h * 128 + 128].T.astype(BF16)
            for t in range(8):
                out_ref[16 + 8 * h + t, at : at + 16, :] = turned[16 * t : 16 * t + 16, :]
    folded = jnp.dot(fold, jnp.concatenate(minuses, axis=1), preferred_element_type=F32).astype(BF16)
    folded = jnp.concatenate([folded[:, n * HALF : n * HALF + HALF] for n in range(4)], axis=0)
    turned = lax.dot_general(turn, folded, (((1,), (1,)), ((), ())), preferred_element_type=F32).astype(BF16)
    for n, at in enumerate(places):
        for t in range(16):
            out_ref[t, at : at + 16, :] = turned[16 * t : 16 * t + 16, n * 128 : n * 128 + 128]
    high = (fy // 256).astype(F32)
    low = (fy % 256).astype(F32)
    tail = jnp.where(iota((8, 128), 0) == 0, high, jnp.where(iota((8, 128), 0) == 1, low, 0.0)).astype(BF16)
    for to in range(32):
        out_ref[to, 64:72, :] = tail


def row_kernel(y_ref, out_ref, tb_ref, acc_ref, e2_ref, e1_ref, fy_ref):
    strip = lax.axis_index("strip")

    def odd_of(rows):
        n = iota((rows, HALF), 1)
        return 2 * (32 * ((n % 128) // 16) + 16 * (n // 128) + n % 16) + 1

    fill_low_table(e2_ref, odd_of(8))
    for f in range(32):
        tail = y_ref[f, 64:72, :].astype(F32)
        fy_ref[f : f + 1, :] = tail[0:1] * 256.0 + tail[1:2]
    fy = fy_ref[...].astype(jnp.int32)
    fy = jnp.concatenate([fy, fy], axis=1)
    e1_t = (2 * (fy + strip * ROWS) + ROWS - 1) * odd_of(32)
    e1_ref[0] = cos_turn(e1_t)
    e1_ref[1] = sin_turn(e1_t)
    per = ROW_BLOCK // 128

    def prepare(b):
        for n in range(per):
            f = b * per + n
            c1 = e1_ref[0, f : f + 1, :]
            s1 = e1_ref[1, f : f + 1, :]
            for r in range(0, 64, STEP):
                c2 = e2_ref[0, r : r + STEP, :]
                s2 = e2_ref[1, r : r + STEP, :]
                to = slice(n * 128 + r, n * 128 + r + STEP)
                tb_ref[b % 2, to, :HALF] = (c1 * c2).astype(BF16)
                tb_ref[b % 2, to, HALF:] = (s1 * c2).astype(BF16)
                to = slice(n * 128 + 64 + r, n * 128 + 64 + r + STEP)
                tb_ref[b % 2, to, :HALF] = (-s1 * s2).astype(BF16)
                tb_ref[b % 2, to, HALF:] = (c1 * s2).astype(BF16)

    prepare(0)
    for b in range(ROW_BLOCKS):
        if b + 1 < ROW_BLOCKS:
            prepare(b + 1)
        left = jnp.concatenate([y_ref[b * per + n, 0:64, :] for n in range(per)], axis=1)
        part = jnp.dot(left, tb_ref[b % 2], preferred_element_type=F32)
        if b == 0:
            acc_ref[...] = part
        else:
            acc_ref[...] += part
    cr = acc_ref[0:32, :HALF]
    sr = acc_ref[0:32, HALF:]
    ci = acc_ref[32:64, :HALF]
    si = acc_ref[32:64, HALF:]
    plus = jnp.concatenate([cr + si, ci - sr], axis=0)
    minus = jnp.concatenate([cr - si, ci + sr], axis=0).astype(BF16)
    minus = jnp.dot(minus, mirror(), preferred_element_type=F32)
    for first, z in ((8, plus), (0, minus)):
        turned = jnp.concatenate([z[:, :128], z[:, 128:]], axis=0).T.astype(BF16)
        for t in range(8):
            out_ref[first + t] = turned[16 * t : 16 * t + 16, :]


def sum_kernel(z_ref, out_ref):
    parts = [z_ref[s].astype(F32) for s in range(16)]
    while len(parts) > 1:
        parts = [a + b for a, b in zip(parts[::2], parts[1::2], strict=True)]
    turned = parts[0].T
    out_ref[:, 0:16] = turned[0:64]
    out_ref[:, 16:32] = turned[64:128]


def vmem():
    return pl.BlockSpec(memory_space=pltpu.VMEM)


def hbm():
    return pl.BlockSpec(memory_space=pltpu.HBM)


def per_device(facet_pixels, facet_offsets, subgrid_offsets):
    limit = pltpu.CompilerParams(vmem_limit_bytes=48 << 20)
    chunks = pl.pallas_call(
        column_kernel,
        out_shape=jax.ShapeDtypeStruct((32, CHUNK_ROWS, 128), BF16),
        in_specs=[hbm(), hbm(), hbm()],
        out_specs=vmem(),
        scratch_shapes=[
            pltpu.VMEM((2, ROWS, WIDTH), BF16),
            pltpu.SMEM((1, 2), jnp.int32),
            pltpu.SMEM((2, 2), jnp.int32),
            pltpu.VMEM((2, 2, 512, BLOCK), BF16),
            pltpu.VMEM((2, BLOCK, 512), BF16),
            pltpu.VMEM((512, 512), F32),
            pltpu.VMEM((2, ROWS, HALF), F32),
            pltpu.VMEM((2, 16, HALF), F32),
            pltpu.VMEM((8, MIDDLE // 2), F32),
            pltpu.SemaphoreType.DMA((2 * BLOCKS + 2,)),
        ],
        compiler_params=limit,
        name="column_dft",
    )(*(pltpu.with_memory_space_constraint(a, pltpu.HBM) for a in (facet_pixels, facet_offsets, subgrid_offsets)))
    chunks = lax.all_to_all(chunks, "facet", 0, 0, tiled=True)
    parts = pl.pallas_call(
        row_kernel,
        out_shape=jax.ShapeDtypeStruct((16, 16, 128), BF16),
        in_specs=[vmem()],
        out_specs=vmem(),
        scratch_shapes=[
            pltpu.VMEM((2, ROW_BLOCK, 512), BF16),
            pltpu.VMEM((64, 512), F32),
            pltpu.VMEM((2, ROWS // 2, HALF), F32),
            pltpu.VMEM((2, 32, HALF), F32),
            pltpu.VMEM((32, 128), F32),
        ],
        compiler_params=limit,
        name="row_dft",
    )(chunks)
    parts = lax.all_to_all(parts, "strip", 0, 0, tiled=True)
    out = pl.pallas_call(
        sum_kernel,
        out_shape=jax.ShapeDtypeStruct((64, 32), F32),
        in_specs=[vmem()],
        out_specs=vmem(),
        name="strip_sum",
    )(pltpu.with_memory_space_constraint(parts, pltpu.VMEM))
    return jnp.transpose(out.reshape(2, 2, 16, 32), (3, 0, 1, 2))


def solution(mesh):
    in_specs = (P(None, "facet", "strip", None), P("facet", None), P())
    out_specs = P("strip", None, None, "facet")
    return jax.shard_map(
        per_device, mesh=mesh, in_specs=in_specs, out_specs=out_specs, check_vma=False
    )
```

```python
import math

import jax
import jax.numpy as jnp
from jax import lax
from jax.experimental import pallas as pl
from jax.experimental.pallas import tpu as pltpu
from jax.sharding import PartitionSpec as P

TURN = 262144
HALF = 256
FREQ = 512
COLUMNS = 2
ROWS = 128
WIDTH = 4096
MIDDLE = WIDTH // 2
BLOCK = 512
BLOCKS = MIDDLE // BLOCK
ROW_BLOCK = 512
ROW_BLOCKS = 32 * ROWS // ROW_BLOCK

STEP = 16
XSTEP = 32
F32 = jnp.float32
BF16 = jnp.bfloat16


def cos_turn(t):
    v = jnp.abs((t & (TURN - 1)) - TURN // 2) - TURN // 4
    z = v.astype(F32) * (2.0 * math.pi / TURN)
    q = z * z
    p = -1.0 / 39916800.0
    for term in (1.0 / 362880.0, -1.0 / 5040.0, 1.0 / 120.0, -1.0 / 6.0):
        p = p * q + term
    return z + z * (q * p)


def sin_turn(t):
    return cos_turn(t - TURN // 4)


def iota(shape, axis):
    return lax.broadcasted_iota(jnp.int32, shape, axis)


def fill_low_table(e2_ref, odd):
    q_t = (2 * iota((8, HALF), 0) + 1) * odd
    p_t = iota((16, HALF), 0) * (16 * odd[0:1])
    qc, qs, pc, ps = cos_turn(q_t), sin_turn(q_t), cos_turn(p_t), sin_turn(p_t)
    for p in range(e2_ref.shape[1] // 8):
        c1, s1 = pc[p : p + 1], ps[p : p + 1]
        e2_ref[0, 8 * p : 8 * p + 8, :] = c1 * qc - s1 * qs
        e2_ref[1, 8 * p : 8 * p + 8, :] = s1 * qc + c1 * qs


def fill_block(tb_ref, slot, n, e1_ref, at, e2_ref):
    c1 = e1_ref[0, at : at + 1, :]
    s1 = e1_ref[1, at : at + 1, :]
    for r in range(0, ROWS, STEP):
        c2 = e2_ref[0, r : r + STEP, :]
        s2 = e2_ref[1, r : r + STEP, :]
        to = slice(n * 128 + r, n * 128 + r + STEP)
        tb_ref[slot, to, :HALF] = (c1 * c2 - s1 * s2).astype(BF16)
        tb_ref[slot, to, HALF:] = (s1 * c2 + c1 * s2).astype(BF16)


def mirror():
    return (iota((HALF, HALF), 0) + iota((HALF, HALF), 1) == HALF - 1).astype(BF16)


def column_kernel(
    x_hbm, facet_hbm, sub_hbm, out_ref, x_ref, facet_ref, sub_ref, xp_ref, tb_ref, acc_ref, e2_ref, e1_ref, tw_ref, sems
):
    small = [
        pltpu.make_async_copy(facet_hbm, facet_ref, sems.at[2 * BLOCKS]),
        pltpu.make_async_copy(sub_hbm, sub_ref, sems.at[2 * BLOCKS + 1]),
    ]
    copies = []
    for b in range(BLOCKS):
        for side, lo in enumerate((MIDDLE + b * BLOCK, MIDDLE - (b + 1) * BLOCK)):
            span = pl.ds(lo, BLOCK)
            copies.append(
                pltpu.make_async_copy(x_hbm.at[:, 0, :, span], x_ref.at[:, :, span], sems.at[2 * b + side])
            )
    for copy in small + copies:
        copy.start()
    strip = lax.axis_index("strip")
    odd = 2 * iota((8, HALF), 1) + 1
    fill_low_table(e2_ref, odd)
    e1_t = iota((16, HALF), 0) * (256 * (2 * iota((16, HALF), 1) + 1))
    e1_ref[0] = cos_turn(e1_t)
    e1_ref[1] = sin_turn(e1_t)
    for copy in small:
        copy.wait()
    fx = facet_ref[0, 0]
    fy = facet_ref[0, 1]
    row = iota((8, MIDDLE // 2), 0)
    centre = jnp.where(row % 2 == 0, 2 * sub_ref[0, 0] + 511, 2 * sub_ref[1, 0] + 511)
    odd_pixel = 2 * (iota((8, MIDDLE // 2), 1) + jnp.where(row >= 4, MIDDLE // 2, 0)) + 1
    tw_ref[...] = cos_turn(odd_pixel * centre - jnp.where(row % 4 >= 2, TURN // 4, 0))
    turn = mirror()

    def prepare(b, pairs):
        if 0 in pairs:
            copies[2 * b].wait()
            copies[2 * b + 1].wait()
        slot = b % 2
        for pair in pairs:
            low = MIDDLE - b * BLOCK - 256 * (pair + 1)
            turned = [
                jnp.dot(x_ref[part, :, low : low + 256], turn, preferred_element_type=F32) for part in range(2)
            ]
            for n in range(2 * pair, 2 * pair + 2):
                lo = b * BLOCK + n * 128
                half, at = 4 * (lo // (MIDDLE // 2)), lo % (MIDDLE // 2)
                to = slice(n * 128, n * 128 + 128)
                side = slice(128 * (n % 2), 128 * (n % 2) + 128)
                turns = [
                    [tw_ref[half + q + c : half + q + c + 1, at : at + 128] for q in (0, 2)] for c in range(COLUMNS)
                ]
                for r in range(0, ROWS, XSTEP):
                    up = slice(MIDDLE + lo, MIDDLE + lo + 128)
                    ar = x_ref[0, r : r + XSTEP, up].astype(F32)
                    ai = x_ref[1, r : r + XSTEP, up].astype(F32)
                    br = turned[0][r : r + XSTEP, side]
                    bi = turned[1][r : r + XSTEP, side]
                    pr, pi, qr, qi = ar + br, ai + bi, ar - br, ai - bi
                    for c, (wc, ws) in enumerate(turns):
                        row = c * 2 * ROWS + r
                        xp_ref[slot, 0, row : row + XSTEP, to] = (pr * wc + qi * ws).astype(BF16)
                        xp_ref[slot, 1, row : row + XSTEP, to] = (qr * wc + pi * ws).astype(BF16)
                        row += ROWS
                        xp_ref[slot, 0, row : row + XSTEP, to] = (pi * wc - qr * ws).astype(BF16)
                        xp_ref[slot, 1, row : row + XSTEP, to] = (qi * wc - pr * ws).astype(BF16)
                fill_block(tb_ref, slot, n, e1_ref, lo // 128, e2_ref)

    pairs = BLOCK // 256
    prepare(0, range(pairs))
    for b in range(BLOCKS):
        for h in range(2):
            if b + 1 < BLOCKS:
                prepare(b + 1, range(h * pairs // 2, (h + 1) * pairs // 2))
            cols = slice(h * HALF, h * HALF + HALF)
            part = jnp.dot(xp_ref[b % 2, h], tb_ref[b % 2, :, cols], preferred_element_type=F32)
            if b == 0:
                acc_ref[:, cols] = part
            else:
                acc_ref[:, cols] += part

    to, at = iota((ROWS, ROWS), 0), iota((ROWS, ROWS), 1)
    lower = (at == 63 - to % 64).astype(F32)
    fold = ((at == 64 + to % 64).astype(F32) + jnp.where(to < 64, lower, -lower)).astype(BF16)
    psi_t = (2 * fx + WIDTH - 1) * odd
    cpsi = cos_turn(psi_t)[0:1]
    spsi = sin_turn(psi_t)[0:1]
    scale = 1.0 / 16384.0
    places, pluses, minuses = [], [], []
    for c in range(COLUMNS):
        step = 2 * (2 * sub_ref[c, 1] + 511)
        q_t = (fy + strip * ROWS + iota((8, 128), 0)) * step + (2 * fx + WIDTH - 1) * (
            2 * sub_ref[c, 0] + 511
        )
        p_t = iota((16, 128), 0) * (8 * step)
        qc, qs, pc, ps = cos_turn(q_t) * scale, sin_turn(q_t) * scale, cos_turn(p_t), sin_turn(p_t)
        cphi = jnp.concatenate([pc[p : p + 1] * qc - ps[p : p + 1] * qs for p in range(16)], axis=0)
        sphi = jnp.concatenate([ps[p : p + 1] * qc + pc[p : p + 1] * qs for p in range(16)], axis=0)
        base = c * 2 * ROWS
        plus, minus = [[], []], [[], []]
        for lo in range(0, HALF, 128):
            cp, sp = cpsi[:, lo : lo + 128], spsi[:, lo : lo + 128]
            cr = acc_ref[base : base + ROWS, lo : lo + 128]
            sr = acc_ref[base : base + ROWS, HALF + lo : HALF + lo + 128]
            ci = acc_ref[base + ROWS : base + 2 * ROWS, lo : lo + 128]
            si = acc_ref[base + ROWS : base + 2 * ROWS, HALF + lo : HALF + lo + 128]
            cc, ss, sc, cs = cphi * cp, sphi * sp, sphi * cp, cphi * sp
            yr, yi, pc, ps = cr + si, ci - sr, cc - ss, sc + cs
            plus[0].append((yr * pc + yi * ps).astype(BF16))
            plus[1].append((yi * pc - yr * ps).astype(BF16))
            yr, yi, pc, ps = cr - si, ci + sr, cc + ss, sc - cs
            minus[0].append((yr * pc + yi * ps).astype(BF16))
            minus[1].append((yi * pc - yr * ps).astype(BF16))
        for part in range(2):
            places.append((part * 2 + c) * 16)
            pluses.append(jnp.concatenate(plus[part], axis=1))
            minuses.append(jnp.concatenate(minus[part], axis=1))
    folded = jnp.dot(fold, jnp.concatenate(pluses, axis=1), preferred_element_type=F32)
    for n, at in enumerate(places):
        for h in range(2):
            turned = folded[:, n * HALF + h * 128 : n * HALF + h * 128 + 128].T.astype(BF16)
            for t in range(8):
                out_ref[16 + 8 * h + t, at // 2 : at // 2 + 8, :, :] = turned[16 * t : 16 * t + 16, :].reshape(8, 2, 128)
    folded = jnp.dot(fold, jnp.concatenate(minuses, axis=1), preferred_element_type=F32).astype(BF16)
    folded = jnp.concatenate([folded[:, n * HALF : n * HALF + HALF] for n in range(4)], axis=0)
    turned = lax.dot_general(turn, folded, (((1,), (1,)), ((), ())), preferred_element_type=F32).astype(BF16)
    for n, at in enumerate(places):
        for t in range(16):
            out_ref[t, at // 2 : at // 2 + 8, :, :] = turned[16 * t : 16 * t + 16, n * 128 : n * 128 + 128].reshape(8, 2, 128)
    high = (fy // 256).astype(F32)
    low = (fy % 256).astype(F32)
    tail = jnp.where(iota((2, 128), 0) == 0, high, low).astype(BF16)
    for to in range(32):
        out_ref[to, 32, :, :] = tail


def row_kernel(y_ref, out_ref, tb_ref, acc_ref, e2_ref, e1_ref, fy_ref):
    strip = lax.axis_index("strip")

    def odd_of(rows):
        n = iota((rows, HALF), 1)
        return 2 * (32 * ((n % 128) // 16) + 16 * (n // 128) + n % 16) + 1

    fill_low_table(e2_ref, odd_of(8))
    for f in range(32):
        tail = y_ref[f, 32, :, :].astype(F32)
        fy_ref[f : f + 1, :] = tail[0:1] * 256.0 + tail[1:2]
    fy = fy_ref[...].astype(jnp.int32)
    fy = jnp.concatenate([fy, fy], axis=1)
    e1_t = (2 * (fy + strip * ROWS) + ROWS - 1) * odd_of(32)
    e1_ref[0] = cos_turn(e1_t)
    e1_ref[1] = sin_turn(e1_t)
    per = ROW_BLOCK // 128

    def prepare(b):
        for n in range(per):
            f = b * per + n
            c1 = e1_ref[0, f : f + 1, :]
            s1 = e1_ref[1, f : f + 1, :]
            for r in range(0, 64, STEP):
                c2 = e2_ref[0, r : r + STEP, :]
                s2 = e2_ref[1, r : r + STEP, :]
                to = slice(n * 128 + r, n * 128 + r + STEP)
                tb_ref[b % 2, to, :HALF] = (c1 * c2).astype(BF16)
                tb_ref[b % 2, to, HALF:] = (s1 * c2).astype(BF16)
                to = slice(n * 128 + 64 + r, n * 128 + 64 + r + STEP)
                tb_ref[b % 2, to, :HALF] = (-s1 * s2).astype(BF16)
                tb_ref[b % 2, to, HALF:] = (c1 * s2).astype(BF16)

    prepare(0)
    for b in range(ROW_BLOCKS):
        if b + 1 < ROW_BLOCKS:
            prepare(b + 1)
        left = jnp.concatenate([y_ref[b * per + n, 0:32, :, :].reshape(64, 128) for n in range(per)], axis=1)
        part = jnp.dot(left, tb_ref[b % 2], preferred_element_type=F32)
        if b == 0:
            acc_ref[...] = part
        else:
            acc_ref[...] += part
    cr = acc_ref[0:32, :HALF]
    sr = acc_ref[0:32, HALF:]
    ci = acc_ref[32:64, :HALF]
    si = acc_ref[32:64, HALF:]
    plus = jnp.concatenate([cr + si, ci - sr], axis=0)
    minus = jnp.concatenate([cr - si, ci + sr], axis=0).astype(BF16)
    minus = jnp.dot(minus, mirror(), preferred_element_type=F32)
    for first, z in ((8, plus), (0, minus)):
        turned = jnp.concatenate([z[:, :128], z[:, 128:]], axis=0).T.astype(BF16)
        for t in range(8):
            out_ref[first + t] = turned[16 * t : 16 * t + 16, :]


def sum_kernel(z_ref, out_ref):
    parts = [z_ref[s].astype(F32) for s in range(16)]
    while len(parts) > 1:
        parts = [a + b for a, b in zip(parts[::2], parts[1::2], strict=True)]
    turned = parts[0].T
    out_ref[:, 0:16] = turned[0:64]
    out_ref[:, 16:32] = turned[64:128]


def vmem():
    return pl.BlockSpec(memory_space=pltpu.VMEM)


def hbm():
    return pl.BlockSpec(memory_space=pltpu.HBM)


def per_device(facet_pixels, facet_offsets, subgrid_offsets):
    limit = pltpu.CompilerParams(vmem_limit_bytes=48 << 20)
    chunks = pl.pallas_call(
        column_kernel,
        out_shape=jax.ShapeDtypeStruct((32, 33, 2, 128), BF16),
        in_specs=[hbm(), hbm(), hbm()],
        out_specs=vmem(),
        scratch_shapes=[
            pltpu.VMEM((2, ROWS, WIDTH), BF16),
            pltpu.SMEM((1, 2), jnp.int32),
            pltpu.SMEM((2, 2), jnp.int32),
            pltpu.VMEM((2, 2, 512, BLOCK), BF16),
            pltpu.VMEM((2, BLOCK, 512), BF16),
            pltpu.VMEM((512, 512), F32),
            pltpu.VMEM((2, ROWS, HALF), F32),
            pltpu.VMEM((2, 16, HALF), F32),
            pltpu.VMEM((8, MIDDLE // 2), F32),
            pltpu.SemaphoreType.DMA((2 * BLOCKS + 2,)),
        ],
        compiler_params=limit,
        name="column_dft",
    )(*(pltpu.with_memory_space_constraint(a, pltpu.HBM) for a in (facet_pixels, facet_offsets, subgrid_offsets)))
    chunks = lax.all_to_all(chunks, "facet", 0, 0, tiled=True)
    parts = pl.pallas_call(
        row_kernel,
        out_shape=jax.ShapeDtypeStruct((16, 16, 128), BF16),
        in_specs=[vmem()],
        out_specs=vmem(),
        scratch_shapes=[
            pltpu.VMEM((2, ROW_BLOCK, 512), BF16),
            pltpu.VMEM((64, 512), F32),
            pltpu.VMEM((2, ROWS // 2, HALF), F32),
            pltpu.VMEM((2, 32, HALF), F32),
            pltpu.VMEM((32, 128), F32),
        ],
        compiler_params=limit,
        name="row_dft",
    )(chunks)
    parts = lax.all_to_all(parts, "strip", 0, 0, tiled=True)
    out = pl.pallas_call(
        sum_kernel,
        out_shape=jax.ShapeDtypeStruct((64, 32), F32),
        in_specs=[vmem()],
        out_specs=vmem(),
        name="strip_sum",
    )(pltpu.with_memory_space_constraint(parts, pltpu.VMEM))
    return jnp.transpose(out.reshape(2, 2, 16, 32), (3, 0, 1, 2))


def solution(mesh):
    in_specs = (P(None, "facet", "strip", None), P("facet", None), P())
    out_specs = P("strip", None, None, "facet")
    return jax.shard_map(
        per_device, mesh=mesh, in_specs=in_specs, out_specs=out_specs, check_vma=False
    )
```

```python
import math

import jax
import jax.numpy as jnp
from jax import lax
from jax.experimental import pallas as pl
from jax.experimental.pallas import tpu as pltpu
from jax.sharding import PartitionSpec as P

TURN = 262144
HALF = 256
FREQ = 512
COLUMNS = 2
ROWS = 128
WIDTH = 4096
MIDDLE = WIDTH // 2
BLOCK = 512
BLOCKS = MIDDLE // BLOCK
ROW_BLOCK = 512
ROW_BLOCKS = 32 * ROWS // ROW_BLOCK

STEP = 16
XSTEP = 32
F32 = jnp.float32
BF16 = jnp.bfloat16


def cos_turn(t):
    v = jnp.abs((t & (TURN - 1)) - TURN // 2) - TURN // 4
    z = v.astype(F32) * (2.0 * math.pi / TURN)
    q = z * z
    p = -1.0 / 39916800.0
    for term in (1.0 / 362880.0, -1.0 / 5040.0, 1.0 / 120.0, -1.0 / 6.0):
        p = p * q + term
    return z + z * (q * p)


def sin_turn(t):
    return cos_turn(t - TURN // 4)


def iota(shape, axis):
    return lax.broadcasted_iota(jnp.int32, shape, axis)


def fill_low_table(e2_ref, odd):
    q_t = (2 * iota((8, HALF), 0) + 1) * odd
    p_t = iota((16, HALF), 0) * (16 * odd[0:1])
    qc, qs, pc, ps = cos_turn(q_t), sin_turn(q_t), cos_turn(p_t), sin_turn(p_t)
    for p in range(e2_ref.shape[1] // 8):
        c1, s1 = pc[p : p + 1], ps[p : p + 1]
        e2_ref[0, 8 * p : 8 * p + 8, :] = c1 * qc - s1 * qs
        e2_ref[1, 8 * p : 8 * p + 8, :] = s1 * qc + c1 * qs


def fill_block(tb_ref, slot, n, e1_ref, at, e2_ref):
    c1 = e1_ref[0, at : at + 1, :]
    s1 = e1_ref[1, at : at + 1, :]
    for r in range(0, ROWS, STEP):
        c2 = e2_ref[0, r : r + STEP, :]
        s2 = e2_ref[1, r : r + STEP, :]
        to = slice(n * 128 + r, n * 128 + r + STEP)
        tb_ref[slot, to, :HALF] = (c1 * c2 - s1 * s2).astype(BF16)
        tb_ref[slot, to, HALF:] = (s1 * c2 + c1 * s2).astype(BF16)


def mirror():
    return (iota((HALF, HALF), 0) + iota((HALF, HALF), 1) == HALF - 1).astype(BF16)


def column_kernel(
    x_hbm, facet_hbm, sub_hbm, out_ref, x_ref, facet_ref, sub_ref, xp_ref, tb_ref, acc_ref, e2_ref, e1_ref, tw_ref, fold_ref, sems
):
    small = [
        pltpu.make_async_copy(facet_hbm, facet_ref, sems.at[2 * BLOCKS]),
        pltpu.make_async_copy(sub_hbm, sub_ref, sems.at[2 * BLOCKS + 1]),
    ]
    copies = []
    for b in range(BLOCKS):
        for side, lo in enumerate((MIDDLE + b * BLOCK, MIDDLE - (b + 1) * BLOCK)):
            span = pl.ds(lo, BLOCK)
            copies.append(
                pltpu.make_async_copy(x_hbm.at[:, 0, :, span], x_ref.at[:, :, span], sems.at[2 * b + side])
            )
    for copy in small + copies:
        copy.start()
    strip = lax.axis_index("strip")
    odd = 2 * iota((8, HALF), 1) + 1
    fill_low_table(e2_ref, odd)
    e1_t = iota((16, HALF), 0) * (256 * (2 * iota((16, HALF), 1) + 1))
    e1_ref[0] = cos_turn(e1_t)
    e1_ref[1] = sin_turn(e1_t)
    turn = mirror()
    to, at = iota((ROWS, ROWS), 0), iota((ROWS, ROWS), 1)
    lower = (at == 63 - to % 64).astype(F32)
    fold_ref[...] = ((at == 64 + to % 64).astype(F32) + jnp.where(to < 64, lower, -lower)).astype(BF16)
    for n in range(BLOCK // 128):
        fill_block(tb_ref, 0, n, e1_ref, n, e2_ref)
    for copy in small:
        copy.wait()
    fx = facet_ref[0, 0]
    fy = facet_ref[0, 1]
    row = iota((8, MIDDLE // 2), 0)
    centre = jnp.where(row % 2 == 0, 2 * sub_ref[0, 0] + 511, 2 * sub_ref[1, 0] + 511)
    odd_pixel = 2 * (iota((8, MIDDLE // 2), 1) + jnp.where(row >= 4, MIDDLE // 2, 0)) + 1
    tw_ref[...] = cos_turn(odd_pixel * centre - jnp.where(row % 4 >= 2, TURN // 4, 0))

    def prepare(b, pairs):
        if 0 in pairs:
            copies[2 * b].wait()
            copies[2 * b + 1].wait()
        slot = b % 2
        for pair in pairs:
            low = MIDDLE - b * BLOCK - 256 * (pair + 1)
            turned = [
                jnp.dot(x_ref[part, :, low : low + 256], turn, preferred_element_type=F32) for part in range(2)
            ]
            for n in range(2 * pair, 2 * pair + 2):
                lo = b * BLOCK + n * 128
                half, at = 4 * (lo // (MIDDLE // 2)), lo % (MIDDLE // 2)
                to = slice(n * 128, n * 128 + 128)
                side = slice(128 * (n % 2), 128 * (n % 2) + 128)
                turns = [
                    [tw_ref[half + q + c : half + q + c + 1, at : at + 128] for q in (0, 2)] for c in range(COLUMNS)
                ]
                for r in range(0, ROWS, XSTEP):
                    up = slice(MIDDLE + lo, MIDDLE + lo + 128)
                    ar = x_ref[0, r : r + XSTEP, up].astype(F32)
                    ai = x_ref[1, r : r + XSTEP, up].astype(F32)
                    br = turned[0][r : r + XSTEP, side]
                    bi = turned[1][r : r + XSTEP, side]
                    pr, pi, qr, qi = ar + br, ai + bi, ar - br, ai - bi
                    for c, (wc, ws) in enumerate(turns):
                        row = c * 2 * ROWS + r
                        xp_ref[slot, 0, row : row + XSTEP, to] = (pr * wc + qi * ws).astype(BF16)
                        xp_ref[slot, 1, row : row + XSTEP, to] = (qr * wc + pi * ws).astype(BF16)
                        row += ROWS
                        xp_ref[slot, 0, row : row + XSTEP, to] = (pi * wc - qr * ws).astype(BF16)
                        xp_ref[slot, 1, row : row + XSTEP, to] = (qi * wc - pr * ws).astype(BF16)
                if b > 0:
                    fill_block(tb_ref, slot, n, e1_ref, lo // 128, e2_ref)

    pairs = BLOCK // 256
    prepare(0, range(pairs))
    for b in range(BLOCKS):
        for h in range(2):
            if b + 1 < BLOCKS:
                prepare(b + 1, range(h * pairs // 2, (h + 1) * pairs // 2))
            cols = slice(h * HALF, h * HALF + HALF)
            part = jnp.dot(xp_ref[b % 2, h], tb_ref[b % 2, :, cols], preferred_element_type=F32)
            if b == 0:
                acc_ref[:, cols] = part
            else:
                acc_ref[:, cols] += part

    psi_t = (2 * fx + WIDTH - 1) * odd
    cpsi = cos_turn(psi_t)[0:1]
    spsi = sin_turn(psi_t)[0:1]
    scale = 1.0 / 16384.0
    places, pluses, minuses = [], [], []
    for c in range(COLUMNS):
        step = 2 * (2 * sub_ref[c, 1] + 511)
        q_t = (fy + strip * ROWS + iota((8, 128), 0)) * step + (2 * fx + WIDTH - 1) * (
            2 * sub_ref[c, 0] + 511
        )
        p_t = iota((16, 128), 0) * (8 * step)
        qc, qs, pc, ps = cos_turn(q_t) * scale, sin_turn(q_t) * scale, cos_turn(p_t), sin_turn(p_t)
        cphi = jnp.concatenate([pc[p : p + 1] * qc - ps[p : p + 1] * qs for p in range(16)], axis=0)
        sphi = jnp.concatenate([ps[p : p + 1] * qc + pc[p : p + 1] * qs for p in range(16)], axis=0)
        base = c * 2 * ROWS
        plus, minus = [[], []], [[], []]
        for lo in range(0, HALF, 128):
            cp, sp = cpsi[:, lo : lo + 128], spsi[:, lo : lo + 128]
            cr = acc_ref[base : base + ROWS, lo : lo + 128]
            sr = acc_ref[base : base + ROWS, HALF + lo : HALF + lo + 128]
            ci = acc_ref[base + ROWS : base + 2 * ROWS, lo : lo + 128]
            si = acc_ref[base + ROWS : base + 2 * ROWS, HALF + lo : HALF + lo + 128]
            cc, ss, sc, cs = cphi * cp, sphi * sp, sphi * cp, cphi * sp
            yr, yi, pc, ps = cr + si, ci - sr, cc - ss, sc + cs
            plus[0].append((yr * pc + yi * ps).astype(BF16))
            plus[1].append((yi * pc - yr * ps).astype(BF16))
            yr, yi, pc, ps = cr - si, ci + sr, cc + ss, sc - cs
            minus[0].append((yr * pc + yi * ps).astype(BF16))
            minus[1].append((yi * pc - yr * ps).astype(BF16))
        for part in range(2):
            places.append((part * 2 + c) * 16)
            pluses.append(jnp.concatenate(plus[part], axis=1))
            minuses.append(jnp.concatenate(minus[part], axis=1))
    folded = jnp.dot(fold_ref[...], jnp.concatenate(pluses, axis=1), preferred_element_type=F32)
    for n, at in enumerate(places):
        for h in range(2):
            turned = folded[:, n * HALF + h * 128 : n * HALF + h * 128 + 128].T.astype(BF16)
            for t in range(8):
                out_ref[16 + 8 * h + t, at // 2 : at // 2 + 8, :, :] = turned[16 * t : 16 * t + 16, :].reshape(8, 2, 128)
    folded = jnp.dot(fold_ref[...], jnp.concatenate(minuses, axis=1), preferred_element_type=F32).astype(BF16)
    folded = jnp.concatenate([folded[:, n * HALF : n * HALF + HALF] for n in range(4)], axis=0)
    turned = lax.dot_general(turn, folded, (((1,), (1,)), ((), ())), preferred_element_type=F32).astype(BF16)
    for n, at in enumerate(places):
        for t in range(16):
            out_ref[t, at // 2 : at // 2 + 8, :, :] = turned[16 * t : 16 * t + 16, n * 128 : n * 128 + 128].reshape(8, 2, 128)
    high = (fy // 256).astype(F32)
    low = (fy % 256).astype(F32)
    tail = jnp.where(iota((2, 128), 0) == 0, high, low).astype(BF16)
    for to in range(32):
        out_ref[to, 32, :, :] = tail


def row_kernel(y_ref, out_ref, tb_ref, acc_ref, e2_ref, e1_ref, fy_ref):
    strip = lax.axis_index("strip")

    def odd_of(rows):
        n = iota((rows, HALF), 1)
        return 2 * (32 * ((n % 128) // 16) + 16 * (n // 128) + n % 16) + 1

    fill_low_table(e2_ref, odd_of(8))
    for f in range(32):
        tail = y_ref[f, 32, :, :].astype(F32)
        fy_ref[f : f + 1, :] = tail[0:1] * 256.0 + tail[1:2]
    fy = fy_ref[...].astype(jnp.int32)
    fy = jnp.concatenate([fy, fy], axis=1)
    e1_t = (2 * (fy + strip * ROWS) + ROWS - 1) * odd_of(32)
    e1_ref[0] = cos_turn(e1_t)
    e1_ref[1] = sin_turn(e1_t)
    per = ROW_BLOCK // 128

    def prepare(b):
        for n in range(per):
            f = b * per + n
            c1 = e1_ref[0, f : f + 1, :]
            s1 = e1_ref[1, f : f + 1, :]
            for r in range(0, 64, STEP):
                c2 = e2_ref[0, r : r + STEP, :]
                s2 = e2_ref[1, r : r + STEP, :]
                to = slice(n * 128 + r, n * 128 + r + STEP)
                tb_ref[b % 2, to, :HALF] = (c1 * c2).astype(BF16)
                tb_ref[b % 2, to, HALF:] = (s1 * c2).astype(BF16)
                to = slice(n * 128 + 64 + r, n * 128 + 64 + r + STEP)
                tb_ref[b % 2, to, :HALF] = (-s1 * s2).astype(BF16)
                tb_ref[b % 2, to, HALF:] = (c1 * s2).astype(BF16)

    prepare(0)
    for b in range(ROW_BLOCKS):
        if b + 1 < ROW_BLOCKS:
            prepare(b + 1)
        left = jnp.concatenate([y_ref[b * per + n, 0:32, :, :].reshape(64, 128) for n in range(per)], axis=1)
        part = jnp.dot(left, tb_ref[b % 2], preferred_element_type=F32)
        if b == 0:
            acc_ref[...] = part
        else:
            acc_ref[...] += part
    cr = acc_ref[0:32, :HALF]
    sr = acc_ref[0:32, HALF:]
    ci = acc_ref[32:64, :HALF]
    si = acc_ref[32:64, HALF:]
    plus = jnp.concatenate([cr + si, ci - sr], axis=0)
    minus = jnp.concatenate([cr - si, ci + sr], axis=0).astype(BF16)
    minus = jnp.dot(minus, mirror(), preferred_element_type=F32)
    for first, z in ((8, plus), (0, minus)):
        turned = jnp.concatenate([z[:, :128], z[:, 128:]], axis=0).T.astype(BF16)
        for t in range(8):
            out_ref[first + t] = turned[16 * t : 16 * t + 16, :]


def sum_kernel(z_ref, out_ref):
    parts = [z_ref[s].astype(F32) for s in range(16)]
    while len(parts) > 1:
        parts = [a + b for a, b in zip(parts[::2], parts[1::2], strict=True)]
    turned = parts[0].T
    out_ref[:, 0:16] = turned[0:64]
    out_ref[:, 16:32] = turned[64:128]


def vmem():
    return pl.BlockSpec(memory_space=pltpu.VMEM)


def hbm():
    return pl.BlockSpec(memory_space=pltpu.HBM)


def per_device(facet_pixels, facet_offsets, subgrid_offsets):
    limit = pltpu.CompilerParams(vmem_limit_bytes=48 << 20)
    chunks = pl.pallas_call(
        column_kernel,
        out_shape=jax.ShapeDtypeStruct((32, 33, 2, 128), BF16),
        in_specs=[hbm(), hbm(), hbm()],
        out_specs=vmem(),
        scratch_shapes=[
            pltpu.VMEM((2, ROWS, WIDTH), BF16),
            pltpu.SMEM((1, 2), jnp.int32),
            pltpu.SMEM((2, 2), jnp.int32),
            pltpu.VMEM((2, 2, 512, BLOCK), BF16),
            pltpu.VMEM((2, BLOCK, 512), BF16),
            pltpu.VMEM((512, 512), F32),
            pltpu.VMEM((2, ROWS, HALF), F32),
            pltpu.VMEM((2, 16, HALF), F32),
            pltpu.VMEM((8, MIDDLE // 2), F32),
            pltpu.VMEM((ROWS, ROWS), BF16),
            pltpu.SemaphoreType.DMA((2 * BLOCKS + 2,)),
        ],
        compiler_params=limit,
        name="column_dft",
    )(*(pltpu.with_memory_space_constraint(a, pltpu.HBM) for a in (facet_pixels, facet_offsets, subgrid_offsets)))
    chunks = lax.all_to_all(chunks, "facet", 0, 0, tiled=True)
    parts = pl.pallas_call(
        row_kernel,
        out_shape=jax.ShapeDtypeStruct((16, 16, 128), BF16),
        in_specs=[vmem()],
        out_specs=vmem(),
        scratch_shapes=[
            pltpu.VMEM((2, ROW_BLOCK, 512), BF16),
            pltpu.VMEM((64, 512), F32),
            pltpu.VMEM((2, ROWS // 2, HALF), F32),
            pltpu.VMEM((2, 32, HALF), F32),
            pltpu.VMEM((32, 128), F32),
        ],
        compiler_params=limit,
        name="row_dft",
    )(chunks)
    parts = lax.all_to_all(parts, "strip", 0, 0, tiled=True)
    out = pl.pallas_call(
        sum_kernel,
        out_shape=jax.ShapeDtypeStruct((64, 32), F32),
        in_specs=[vmem()],
        out_specs=vmem(),
        name="strip_sum",
    )(pltpu.with_memory_space_constraint(parts, pltpu.VMEM))
    return jnp.transpose(out.reshape(2, 2, 16, 32), (3, 0, 1, 2))


def solution(mesh):
    in_specs = (P(None, "facet", "strip", None), P("facet", None), P())
    out_specs = P("strip", None, None, "facet")
    return jax.shard_map(
        per_device, mesh=mesh, in_specs=in_specs, out_specs=out_specs, check_vma=False
    )
```

```python
import math

import jax
import jax.numpy as jnp
from jax import lax
from jax.experimental import pallas as pl
from jax.experimental.pallas import tpu as pltpu
from jax.sharding import PartitionSpec as P

TURN = 262144
HALF = 256
FREQ = 512
COLUMNS = 2
ROWS = 128
WIDTH = 4096
MIDDLE = WIDTH // 2
BLOCK = 512
BLOCKS = MIDDLE // BLOCK
ROW_BLOCK = 512
ROW_BLOCKS = 32 * ROWS // ROW_BLOCK

STEP = 16
XSTEP = 32
F32 = jnp.float32
BF16 = jnp.bfloat16


def cos_turn(t):
    v = jnp.abs((t & (TURN - 1)) - TURN // 2) - TURN // 4
    z = v.astype(F32) * (2.0 * math.pi / TURN)
    q = z * z
    p = -1.0 / 39916800.0
    for term in (1.0 / 362880.0, -1.0 / 5040.0, 1.0 / 120.0, -1.0 / 6.0):
        p = p * q + term
    return z + z * (q * p)


def sin_turn(t):
    return cos_turn(t - TURN // 4)


def iota(shape, axis):
    return lax.broadcasted_iota(jnp.int32, shape, axis)


def fill_low_table(e2_ref, odd):
    q_t = (2 * iota((8, HALF), 0) + 1) * odd
    p_t = iota((16, HALF), 0) * (16 * odd[0:1])
    qc, qs, pc, ps = cos_turn(q_t), sin_turn(q_t), cos_turn(p_t), sin_turn(p_t)
    for p in range(e2_ref.shape[1] // 8):
        c1, s1 = pc[p : p + 1], ps[p : p + 1]
        e2_ref[0, 8 * p : 8 * p + 8, :] = c1 * qc - s1 * qs
        e2_ref[1, 8 * p : 8 * p + 8, :] = s1 * qc + c1 * qs


def fill_block(tb_ref, slot, n, e1_ref, at, e2_ref):
    c1 = e1_ref[0, at : at + 1, :]
    s1 = e1_ref[1, at : at + 1, :]
    for r in range(0, ROWS, STEP):
        c2 = e2_ref[0, r : r + STEP, :]
        s2 = e2_ref[1, r : r + STEP, :]
        to = slice(n * 128 + r, n * 128 + r + STEP)
        tb_ref[slot, to, :HALF] = (c1 * c2 - s1 * s2).astype(BF16)
        tb_ref[slot, to, HALF:] = (s1 * c2 + c1 * s2).astype(BF16)


def mirror():
    return (iota((HALF, HALF), 0) + iota((HALF, HALF), 1) == HALF - 1).astype(BF16)


def column_kernel(
    x_hbm, facet_hbm, sub_hbm, out_ref, x_ref, facet_ref, sub_ref, xp_ref, tb_ref, acc_ref, e2_ref, e1_ref, tw_ref, fold_ref, sems
):
    small = [
        pltpu.make_async_copy(facet_hbm, facet_ref, sems.at[2 * BLOCKS]),
        pltpu.make_async_copy(sub_hbm, sub_ref, sems.at[2 * BLOCKS + 1]),
    ]
    copies = []
    for b in range(BLOCKS):
        for side, lo in enumerate((MIDDLE + b * BLOCK, MIDDLE - (b + 1) * BLOCK)):
            span = pl.ds(lo, BLOCK)
            copies.append(
                pltpu.make_async_copy(x_hbm.at[:, 0, :, span], x_ref.at[:, :, span], sems.at[2 * b + side])
            )
    for copy in small + copies:
        copy.start()
    strip = lax.axis_index("strip")
    odd = 2 * iota((8, HALF), 1) + 1
    fill_low_table(e2_ref, odd)
    e1_t = iota((16, HALF), 0) * (256 * (2 * iota((16, HALF), 1) + 1))
    e1_ref[0] = cos_turn(e1_t)
    e1_ref[1] = sin_turn(e1_t)
    turn = mirror()
    to, at = iota((ROWS, ROWS), 0), iota((ROWS, ROWS), 1)
    lower = (at == 63 - to % 64).astype(F32)
    fold_ref[...] = ((at == 64 + to % 64).astype(F32) + jnp.where(to < 64, lower, -lower)).astype(BF16)
    for n in range(BLOCK // 128):
        fill_block(tb_ref, 0, n, e1_ref, n, e2_ref)
    for copy in small:
        copy.wait()
    fx = facet_ref[0, 0]
    fy = facet_ref[0, 1]
    row = iota((8, MIDDLE // 2), 0)
    centre = jnp.where(row % 2 == 0, 2 * sub_ref[0, 0] + 511, 2 * sub_ref[1, 0] + 511)
    odd_pixel = 2 * (iota((8, MIDDLE // 2), 1) + jnp.where(row >= 4, MIDDLE // 2, 0)) + 1
    tw_ref[...] = cos_turn(odd_pixel * centre - jnp.where(row % 4 >= 2, TURN // 4, 0))

    def prepare(b, pairs):
        if 0 in pairs:
            copies[2 * b].wait()
            copies[2 * b + 1].wait()
        slot = b % 2
        for pair in pairs:
            low = MIDDLE - b * BLOCK - 256 * (pair + 1)
            turned = [
                jnp.dot(x_ref[part, :, low : low + 256], turn, preferred_element_type=F32) for part in range(2)
            ]
            for n in range(2 * pair, 2 * pair + 2):
                lo = b * BLOCK + n * 128
                half, at = 4 * (lo // (MIDDLE // 2)), lo % (MIDDLE // 2)
                to = slice(n * 128, n * 128 + 128)
                side = slice(128 * (n % 2), 128 * (n % 2) + 128)
                turns = [
                    [tw_ref[half + q + c : half + q + c + 1, at : at + 128] for q in (0, 2)] for c in range(COLUMNS)
                ]
                for r in range(0, ROWS, XSTEP):
                    up = slice(MIDDLE + lo, MIDDLE + lo + 128)
                    ar = x_ref[0, r : r + XSTEP, up].astype(F32)
                    ai = x_ref[1, r : r + XSTEP, up].astype(F32)
                    br = turned[0][r : r + XSTEP, side]
                    bi = turned[1][r : r + XSTEP, side]
                    pr, pi, qr, qi = ar + br, ai + bi, ar - br, ai - bi
                    for c, (wc, ws) in enumerate(turns):
                        row = c * 2 * ROWS + r
                        xp_ref[slot, 0, row : row + XSTEP, to] = (pr * wc + qi * ws).astype(BF16)
                        xp_ref[slot, 1, row : row + XSTEP, to] = (qr * wc + pi * ws).astype(BF16)
                        row += ROWS
                        xp_ref[slot, 0, row : row + XSTEP, to] = (pi * wc - qr * ws).astype(BF16)
                        xp_ref[slot, 1, row : row + XSTEP, to] = (qi * wc - pr * ws).astype(BF16)
                if b > 0:
                    fill_block(tb_ref, slot, n, e1_ref, lo // 128, e2_ref)

    pairs = BLOCK // 256
    prepare(0, range(pairs))
    for b in range(BLOCKS):
        for h in range(2):
            cols = slice(h * HALF, h * HALF + HALF)
            part = jnp.dot(xp_ref[b % 2, h], tb_ref[b % 2, :, cols], preferred_element_type=F32)
            if b == 0:
                acc_ref[:, cols] = part
            else:
                acc_ref[:, cols] += part
            if b + 1 < BLOCKS:
                prepare(b + 1, range(h * pairs // 2, (h + 1) * pairs // 2))

    psi_t = (2 * fx + WIDTH - 1) * odd
    cpsi = cos_turn(psi_t)[0:1]
    spsi = sin_turn(psi_t)[0:1]
    scale = 1.0 / 16384.0
    places, pluses, minuses = [], [], []
    for c in range(COLUMNS):
        step = 2 * (2 * sub_ref[c, 1] + 511)
        q_t = (fy + strip * ROWS + iota((8, 128), 0)) * step + (2 * fx + WIDTH - 1) * (
            2 * sub_ref[c, 0] + 511
        )
        p_t = iota((16, 128), 0) * (8 * step)
        qc, qs, pc, ps = cos_turn(q_t) * scale, sin_turn(q_t) * scale, cos_turn(p_t), sin_turn(p_t)
        cphi = jnp.concatenate([pc[p : p + 1] * qc - ps[p : p + 1] * qs for p in range(16)], axis=0)
        sphi = jnp.concatenate([ps[p : p + 1] * qc + pc[p : p + 1] * qs for p in range(16)], axis=0)
        base = c * 2 * ROWS
        plus, minus = [[], []], [[], []]
        for lo in range(0, HALF, 128):
            cp, sp = cpsi[:, lo : lo + 128], spsi[:, lo : lo + 128]
            cr = acc_ref[base : base + ROWS, lo : lo + 128]
            sr = acc_ref[base : base + ROWS, HALF + lo : HALF + lo + 128]
            ci = acc_ref[base + ROWS : base + 2 * ROWS, lo : lo + 128]
            si = acc_ref[base + ROWS : base + 2 * ROWS, HALF + lo : HALF + lo + 128]
            cc, ss, sc, cs = cphi * cp, sphi * sp, sphi * cp, cphi * sp
            yr, yi, pc, ps = cr + si, ci - sr, cc - ss, sc + cs
            plus[0].append((yr * pc + yi * ps).astype(BF16))
            plus[1].append((yi * pc - yr * ps).astype(BF16))
            yr, yi, pc, ps = cr - si, ci + sr, cc + ss, sc - cs
            minus[0].append((yr * pc + yi * ps).astype(BF16))
            minus[1].append((yi * pc - yr * ps).astype(BF16))
        for part in range(2):
            places.append((part * 2 + c) * 16)
            pluses.append(jnp.concatenate(plus[part], axis=1))
            minuses.append(jnp.concatenate(minus[part], axis=1))
    folded = jnp.dot(fold_ref[...], jnp.concatenate(pluses, axis=1), preferred_element_type=F32)
    for n, at in enumerate(places):
        for h in range(2):
            turned = folded[:, n * HALF + h * 128 : n * HALF + h * 128 + 128].T.astype(BF16)
            for t in range(8):
                out_ref[16 + 8 * h + t, at // 2 : at // 2 + 8, :, :] = turned[16 * t : 16 * t + 16, :].reshape(8, 2, 128)
    folded = jnp.dot(fold_ref[...], jnp.concatenate(minuses, axis=1), preferred_element_type=F32).astype(BF16)
    folded = jnp.concatenate([folded[:, n * HALF : n * HALF + HALF] for n in range(4)], axis=0)
    turned = lax.dot_general(turn, folded, (((1,), (1,)), ((), ())), preferred_element_type=F32).astype(BF16)
    for n, at in enumerate(places):
        for t in range(16):
            out_ref[t, at // 2 : at // 2 + 8, :, :] = turned[16 * t : 16 * t + 16, n * 128 : n * 128 + 128].reshape(8, 2, 128)
    high = (fy // 256).astype(F32)
    low = (fy % 256).astype(F32)
    tail = jnp.where(iota((2, 128), 0) == 0, high, low).astype(BF16)
    for to in range(32):
        out_ref[to, 32, :, :] = tail


def row_kernel(y_ref, out_ref, tb_ref, acc_ref, e2_ref, e1_ref, fy_ref):
    strip = lax.axis_index("strip")

    def odd_of(rows):
        n = iota((rows, HALF), 1)
        return 2 * (32 * ((n % 128) // 16) + 16 * (n // 128) + n % 16) + 1

    fill_low_table(e2_ref, odd_of(8))
    for f in range(32):
        tail = y_ref[f, 32, :, :].astype(F32)
        fy_ref[f : f + 1, :] = tail[0:1] * 256.0 + tail[1:2]
    fy = fy_ref[...].astype(jnp.int32)
    fy = jnp.concatenate([fy, fy], axis=1)
    e1_t = (2 * (fy + strip * ROWS) + ROWS - 1) * odd_of(32)
    e1_ref[0] = cos_turn(e1_t)
    e1_ref[1] = sin_turn(e1_t)
    per = ROW_BLOCK // 128

    def prepare(b):
        for n in range(per):
            f = b * per + n
            c1 = e1_ref[0, f : f + 1, :]
            s1 = e1_ref[1, f : f + 1, :]
            for r in range(0, 64, STEP):
                c2 = e2_ref[0, r : r + STEP, :]
                s2 = e2_ref[1, r : r + STEP, :]
                to = slice(n * 128 + r, n * 128 + r + STEP)
                tb_ref[b % 2, to, :HALF] = (c1 * c2).astype(BF16)
                tb_ref[b % 2, to, HALF:] = (s1 * c2).astype(BF16)
                to = slice(n * 128 + 64 + r, n * 128 + 64 + r + STEP)
                tb_ref[b % 2, to, :HALF] = (-s1 * s2).astype(BF16)
                tb_ref[b % 2, to, HALF:] = (c1 * s2).astype(BF16)

    prepare(0)
    for b in range(ROW_BLOCKS):
        if b + 1 < ROW_BLOCKS:
            prepare(b + 1)
        left = jnp.concatenate([y_ref[b * per + n, 0:32, :, :].reshape(64, 128) for n in range(per)], axis=1)
        part = jnp.dot(left, tb_ref[b % 2], preferred_element_type=F32)
        if b == 0:
            acc_ref[...] = part
        else:
            acc_ref[...] += part
    cr = acc_ref[0:32, :HALF]
    sr = acc_ref[0:32, HALF:]
    ci = acc_ref[32:64, :HALF]
    si = acc_ref[32:64, HALF:]
    plus = jnp.concatenate([cr + si, ci - sr], axis=0)
    minus = jnp.concatenate([cr - si, ci + sr], axis=0).astype(BF16)
    minus = jnp.dot(minus, mirror(), preferred_element_type=F32)
    for first, z in ((8, plus), (0, minus)):
        turned = jnp.concatenate([z[:, :128], z[:, 128:]], axis=0).T.astype(BF16)
        for t in range(8):
            out_ref[first + t] = turned[16 * t : 16 * t + 16, :]


def sum_kernel(z_ref, out_ref):
    parts = [z_ref[s].astype(F32) for s in range(16)]
    while len(parts) > 1:
        parts = [a + b for a, b in zip(parts[::2], parts[1::2], strict=True)]
    turned = parts[0].T
    out_ref[:, 0:16] = turned[0:64]
    out_ref[:, 16:32] = turned[64:128]


def vmem():
    return pl.BlockSpec(memory_space=pltpu.VMEM)


def hbm():
    return pl.BlockSpec(memory_space=pltpu.HBM)


def per_device(facet_pixels, facet_offsets, subgrid_offsets):
    limit = pltpu.CompilerParams(vmem_limit_bytes=48 << 20)
    chunks = pl.pallas_call(
        column_kernel,
        out_shape=jax.ShapeDtypeStruct((32, 33, 2, 128), BF16),
        in_specs=[hbm(), hbm(), hbm()],
        out_specs=vmem(),
        scratch_shapes=[
            pltpu.VMEM((2, ROWS, WIDTH), BF16),
            pltpu.SMEM((1, 2), jnp.int32),
            pltpu.SMEM((2, 2), jnp.int32),
            pltpu.VMEM((2, 2, 512, BLOCK), BF16),
            pltpu.VMEM((2, BLOCK, 512), BF16),
            pltpu.VMEM((512, 512), F32),
            pltpu.VMEM((2, ROWS, HALF), F32),
            pltpu.VMEM((2, 16, HALF), F32),
            pltpu.VMEM((8, MIDDLE // 2), F32),
            pltpu.VMEM((ROWS, ROWS), BF16),
            pltpu.SemaphoreType.DMA((2 * BLOCKS + 2,)),
        ],
        compiler_params=limit,
        name="column_dft",
    )(*(pltpu.with_memory_space_constraint(a, pltpu.HBM) for a in (facet_pixels, facet_offsets, subgrid_offsets)))
    chunks = lax.all_to_all(chunks, "facet", 0, 0, tiled=True)
    parts = pl.pallas_call(
        row_kernel,
        out_shape=jax.ShapeDtypeStruct((16, 16, 128), BF16),
        in_specs=[vmem()],
        out_specs=vmem(),
        scratch_shapes=[
            pltpu.VMEM((2, ROW_BLOCK, 512), BF16),
            pltpu.VMEM((64, 512), F32),
            pltpu.VMEM((2, ROWS // 2, HALF), F32),
            pltpu.VMEM((2, 32, HALF), F32),
            pltpu.VMEM((32, 128), F32),
        ],
        compiler_params=limit,
        name="row_dft",
    )(chunks)
    parts = lax.all_to_all(parts, "strip", 0, 0, tiled=True)
    out = pl.pallas_call(
        sum_kernel,
        out_shape=jax.ShapeDtypeStruct((64, 32), F32),
        in_specs=[vmem()],
        out_specs=vmem(),
        name="strip_sum",
    )(pltpu.with_memory_space_constraint(parts, pltpu.VMEM))
    return jnp.transpose(out.reshape(2, 2, 16, 32), (3, 0, 1, 2))


def solution(mesh):
    in_specs = (P(None, "facet", "strip", None), P("facet", None), P())
    out_specs = P("strip", None, None, "facet")
    return jax.shard_map(
        per_device, mesh=mesh, in_specs=in_specs, out_specs=out_specs, check_vma=False
    )
```
